256 devices in a mesh: dp: 4 (over y), expert: 64 (over z, x, core).
Axes of the slice: x: 4, y: 4, z: 8, core: 2. Of those that a mesh axis runs over, the one named last changes fastest.
Arguments:
- tokens: bfloat16 [32768, 3584], P(('dp', 'expert')), may hold values from -24 to 24
- cotangent: bfloat16 [32768, 3584], P(('dp', 'expert')), may hold values from -0.375 to 0.375
- gate_scale: float32 [32768], P(('dp', 'expert')), may hold values from 0.2 to 1
- expert_index: int32 [32768], P(('dp', 'expert')), may hold values from 0 to 63, as said below
- hot_index: int32 [64], replicated, may hold values from 0 to 63, as said below
- w_gate: bfloat16 [64, 3584, 1024], P('expert', None, 'dp'), may hold values from -0.09375 to 0.09375
- w_up: bfloat16 [64, 3584, 1024], P('expert', None, 'dp'), may hold values from -0.09375 to 0.09375
- w_down: bfloat16 [64, 1024, 3584], P('expert', 'dp'), may hold values from -0.1875 to 0.1875
Outputs:
- grad_gate: bfloat16 [64, 3584, 1024], P('expert', None, 'dp')
- grad_up: bfloat16 [64, 3584, 1024], P('expert', None, 'dp')
- grad_down: bfloat16 [64, 1024, 3584], P('expert', 'dp')
- hot_grads: bfloat16 [1, 3584, 3, 1024], P(None, 'expert', None, 'dp')
The draws below stay inside these ranges and needn't reach their ends.
Inputs may be any that keep to these rules, and one draw needn't show every extreme that they name: `expert_index`: among the 128 tokens of one device (aligned blocks of rows), at most 3 are routed to any one expert other than hot_index[0], and from 3 to 6 to hot_index[0]. In every draw each group of devices sharing a dp index has an expert that receives exactly 3 tokens from each of its devices, and some devices route exactly 6 tokens to hot_index[0]. `hot_index`: A permutation of the 64 experts; its first entry is the replicated expert, to which every device routes at least as many tokens as to any other expert.
All inputs are finite; a program needn't handle non-finite values.
Results may differ from the reference program's by a relative error of at most 0.0058.
Values may be sent and summed in bfloat16 or wider, within the bound.
A program may use at most 128 MiB of HBM per device.

```python
import jax
import jax.numpy as jnp
from jax import lax

D = 3584
FF = 1024
TOK_DEV = 128
EXPERTS = 64
TOKENS = 32768
CAP = 3
CAP_HOT = 6


def routing_plan(key):
    blocks = TOKENS // TOK_DEV
    row_groups = blocks // EXPERTS
    order = jax.random.permutation(jax.random.fold_in(key, 101), EXPERTS).astype(jnp.int32)
    hot_expert = order[0]
    full_shift = jax.random.randint(jax.random.fold_in(key, 102), (row_groups,), 0, EXPERTS - 1).astype(jnp.int32)
    full_expert = (hot_expert + 1 + full_shift) % EXPERTS
    forced_row = jax.random.randint(jax.random.fold_in(key, 103), (), 0, row_groups).astype(jnp.int32)
    block_row = jnp.arange(blocks, dtype=jnp.int32) // EXPERTS
    hot_count = jax.random.randint(jax.random.fold_in(key, 104), (blocks,), CAP, CAP_HOT + 1).astype(jnp.int32)
    hot_count = jnp.where(block_row == forced_row, CAP_HOT, hot_count)
    expert_grid = jnp.arange(EXPERTS, dtype=jnp.int32)[None, :, None]
    slot_grid = jnp.arange(CAP_HOT, dtype=jnp.int32)[None, None, :]
    is_hot = expert_grid == hot_expert
    usable = jnp.where(is_hot, slot_grid < hot_count[:, None, None], slot_grid < CAP)
    forced = is_hot & usable | (expert_grid == full_expert[block_row][:, None, None]) & (slot_grid < CAP)
    random_score = jax.random.randint(jax.random.fold_in(key, 105), (blocks, EXPERTS, CAP_HOT), 0, 65536).astype(jnp.int32)
    flat_slot = expert_grid * CAP_HOT + slot_grid
    ranking = (random_score + 131072 * forced.astype(jnp.int32)) * (EXPERTS * CAP_HOT) + flat_slot
    ranking = jnp.where(usable, ranking, -1 - flat_slot)
    chosen = lax.top_k(ranking.reshape(blocks, EXPERTS * CAP_HOT), TOK_DEV)[1].astype(jnp.int32)
    shuffle_key = jax.random.randint(jax.random.fold_in(key, 106), (blocks, TOK_DEV), 0, 65536).astype(jnp.int32)
    shuffle_key = shuffle_key * TOK_DEV + jnp.arange(TOK_DEV, dtype=jnp.int32)[None, :]
    shuffle = jnp.argsort(shuffle_key, axis=1).astype(jnp.int32)
    picked = jnp.take_along_axis(chosen, shuffle, axis=1)
    return (order, (picked // CAP_HOT).reshape(TOKENS).astype(jnp.int32))


def draw_expert_index(key, part):
    return routing_plan(key)[1]


def draw_hot_index(key, part):
    return routing_plan(key)[0]


def with_spikes(drawn, rng, source, target, blocks, factor):
    owner, partner = [(jnp.arange(drawn.shape[axis_at]) // (drawn.shape[axis_at] // blocks)).reshape([-1 if axis == axis_at else 1 for axis in range(drawn.ndim)]) for axis_at in (source, target)]
    chosen = jax.random.permutation(rng, blocks)[partner]
    strong = (owner == chosen) | (owner == (partner + blocks // 2) % blocks)
    return jnp.where(strong, factor * drawn, drawn)


def level_of(rng, dims, cuts, smallest, top_value):
    gain, own = 1.0, jax.random.fold_in(rng, 6)
    for axis_at, blocks in cuts:
        steps = jnp.exp(jax.random.uniform(jax.random.fold_in(own, axis_at), (blocks,), jnp.float32, smallest / len(cuts), top_value / len(cuts)))
        gain = gain * jnp.repeat(steps, dims[axis_at] // blocks).reshape([-1 if axis == axis_at else 1 for axis in range(len(dims))])
    return gain


def scatter_about(rng, shape, spread, limit, shards=(), kind=jnp.bfloat16):
    level = level_of(rng, shape, shards, -0.22, 0.18) if shards else 1.0
    array = jax.random.normal(rng, shape, jnp.float32) * spread * level
    return jnp.minimum(jnp.maximum(array, -limit), limit).astype(kind)


def heavy_noise(own_key, shape, spread, limit, split, heavy, kind=jnp.bfloat16):
    entries = spread * jax.random.normal(own_key, shape, jnp.float32)
    if split:
        entries = entries * level_of(own_key, shape, split, -0.22, 0.18)
    return jnp.clip(with_spikes(entries, jax.random.fold_in(own_key, 3), *heavy), -limit, limit).astype(kind)


def setup_inputs(seed: int = 0) -> dict:
    arg_keys = jax.random.split(jax.random.key(seed), 9)
    tokens = heavy_noise(arg_keys[0], (TOKENS, D), 1.0, 24.0, ((0, 256),), (0, 1, 256, 6.0))
    cotangent = scatter_about(arg_keys[1], (TOKENS, D), 0.0625, 0.375, ((0, 256),))
    gate_scale = jnp.clip(0.2 + 0.8 * jax.random.uniform(arg_keys[2], (TOKENS,), jnp.float32) ** level_of(arg_keys[2], (TOKENS,), ((0, 256),), -0.2, 0.2), 0.2, 1.0)
    expert_index = draw_expert_index(jax.random.fold_in(arg_keys[8], 71), 0)
    hot_index = draw_hot_index(jax.random.fold_in(arg_keys[8], 71), 0)
    w_gate = scatter_about(arg_keys[5], (EXPERTS, D, FF), D ** -0.5, 0.09375, ((0, 64), (2, 4)))
    w_up = scatter_about(arg_keys[6], (EXPERTS, D, FF), D ** -0.5, 0.09375, ((0, 64), (2, 4)))
    w_down = scatter_about(arg_keys[7], (EXPERTS, FF, D), FF ** -0.5, 0.1875, ((0, 64), (1, 4)))
    return dict(tokens=tokens, cotangent=cotangent, gate_scale=gate_scale, expert_index=expert_index, hot_index=hot_index, w_gate=w_gate, w_up=w_up, w_down=w_down)


def expert_terms(row_tokens, row_grads, gate_matrix, up_matrix, down_matrix):
    pre_gate = jnp.dot(row_tokens, gate_matrix, preferred_element_type=jnp.float32)
    pre_up = jnp.dot(row_tokens, up_matrix, preferred_element_type=jnp.float32)
    hidden_back = jnp.dot(row_grads, down_matrix.T, preferred_element_type=jnp.float32)
    sigmoid_gate = jax.nn.sigmoid(pre_gate)
    activated = pre_gate * sigmoid_gate
    hidden = (activated * pre_up).astype(jnp.bfloat16)
    gate_grad = (hidden_back * pre_up * sigmoid_gate * (1.0 + pre_gate * (1.0 - sigmoid_gate))).astype(jnp.bfloat16)
    up_grad = (hidden_back * activated).astype(jnp.bfloat16)
    return hidden, gate_grad, up_grad


def pick_rows(chosen, tokens, route_grad, limit_rows):
    row_index = jnp.nonzero(chosen, size=limit_rows, fill_value=0)[0].astype(jnp.int32)
    live_count = jnp.sum(chosen.astype(jnp.int32))
    is_live = (jnp.arange(limit_rows, dtype=jnp.int32) < live_count)[:, None]
    nothing = jnp.zeros((), tokens.dtype)
    return jnp.where(is_live, tokens[row_index], nothing), jnp.where(is_live, route_grad[row_index], nothing)


def reference(tokens, cotangent, gate_scale, expert_index, hot_index, w_gate, w_up, w_down):
    hot_expert = hot_index[0]
    route_grad = (gate_scale[:, None] * cotangent.astype(jnp.float32)).astype(jnp.bfloat16)
    blocks = TOKENS // TOK_DEV

    def one_expert(expert):
        chosen = (expert_index == expert) & (expert_index != hot_expert)
        row_tokens, row_grads = pick_rows(chosen, tokens, route_grad, CAP * blocks)
        hidden, gate_grad, up_grad = expert_terms(row_tokens, row_grads, w_gate[expert], w_up[expert], w_down[expert])
        gate_total = jnp.dot(row_tokens.T, gate_grad, preferred_element_type=jnp.float32)
        up_total = jnp.dot(row_tokens.T, up_grad, preferred_element_type=jnp.float32)
        down_total = jnp.dot(hidden.T, row_grads, preferred_element_type=jnp.float32)
        return gate_total.astype(jnp.bfloat16), up_total.astype(jnp.bfloat16), down_total.astype(jnp.bfloat16)

    grad_gate, grad_up, grad_down = lax.map(one_expert, jnp.arange(EXPERTS, dtype=jnp.int32))
    row_tokens, row_grads = pick_rows(expert_index == hot_expert, tokens, route_grad, CAP_HOT * blocks)
    hidden, gate_grad, up_grad = expert_terms(row_tokens, row_grads, w_gate[hot_expert], w_up[hot_expert], w_down[hot_expert])
    gate_total = jnp.dot(row_tokens.T, gate_grad, preferred_element_type=jnp.float32)
    up_total = jnp.dot(row_tokens.T, up_grad, preferred_element_type=jnp.float32)
    down_total = jnp.dot(row_grads.T, hidden, preferred_element_type=jnp.float32)
    hot_grads = jnp.stack([gate_total, up_total, down_total], axis=1).astype(jnp.bfloat16)[None]
    return grad_gate, grad_up, grad_down, hot_grads
```

```python
import jax
import jax.numpy as jnp
from jax import lax
from jax.experimental import pallas as pl
from jax.experimental.pallas import tpu as pltpu
from jax.sharding import PartitionSpec as P

CONTRACT_ROWS = (((0,), (0,)), ((), ()))
MESH = pl.DeviceIdType.MESH
PIECES = 8


def spread(block, axis, source):
    block = jnp.where(lax.axis_index(axis) == source, block, jnp.zeros_like(block))
    return lax.psum(block, axis)


def expert_terms(row_tokens, row_grads, gate_matrix, up_matrix, down_matrix):
    pre_gate = jnp.dot(row_tokens, gate_matrix, preferred_element_type=jnp.float32)
    pre_up = jnp.dot(row_tokens, up_matrix, preferred_element_type=jnp.float32)
    hidden_back = lax.dot_general(
        row_grads, down_matrix, (((1,), (1,)), ((), ())), preferred_element_type=jnp.float32
    )
    sigmoid_gate = jax.nn.sigmoid(pre_gate)
    activated = pre_gate * sigmoid_gate
    hidden = (activated * pre_up).astype(jnp.bfloat16)
    gate_grad = (
        hidden_back * pre_up * sigmoid_gate * (1.0 + pre_gate * (1.0 - sigmoid_gate))
    ).astype(jnp.bfloat16)
    up_grad = (hidden_back * activated).astype(jnp.bfloat16)
    return (hidden, gate_grad, up_grad)


def column_sum(left, right):
    return lax.dot_general(left, right, CONTRACT_ROWS, preferred_element_type=jnp.float32)


def route_rows(selector, values):
    return jnp.dot(selector, values, preferred_element_type=jnp.float32).astype(jnp.bfloat16)


def exchange_kernel(nz, nq, send, send_hot, own_hot, got, got_hot, all_hot,
                    mid, mid_hot, z_send, z_recv, q_send, q_recv, local_sem,
                    y_send, y_recv, f_send, f_recv, h_send, h_recv):
    ny = 4
    chunks = send.shape[0]
    y = lax.axis_index("dp")
    e = lax.axis_index("expert")
    z = lax.div(e, nq)
    q = lax.rem(e, nq)
    up = lax.rem(y + 1, ny)
    down = lax.rem(y + ny - 1, ny)

    def z_peer(k):
        return lax.rem(z + k, nz)

    def q_peer(k):
        return lax.rem(q + k, nq)

    def q_source(k):
        return lax.rem(q + nq - k, nq)

    barrier = pltpu.get_barrier_semaphore()
    for k in range(1, nz):
        pl.semaphore_signal(barrier, inc=1, device_id=(y, z_peer(k) * nq + q), device_id_type=MESH)
    for k in range(1, nq):
        pl.semaphore_signal(barrier, inc=1, device_id=(y, z * nq + q_peer(k)), device_id_type=MESH)
    for k in range(1, ny):
        pl.semaphore_signal(barrier, inc=1, device_id=(lax.rem(y + k, ny), e), device_id_type=MESH)
    pl.semaphore_wait(barrier, nz - 1 + nq - 1 + ny - 1)

    def z_refs(s):
        if s < chunks:
            return send.at[s], mid.at[s]
        return send_hot, mid_hot

    def q_dst(s, who):
        if s < chunks:
            return got.at[s, y, who]
        return got_hot.at[:, who, y]

    def y_block(s, who, plane):
        if s < chunks:
            return got.at[s, plane, who]
        return got_hot.at[:, who, plane]

    def z_copy(s, k):
        src, dst = z_refs(s)
        return pltpu.make_async_remote_copy(
            src_ref=src.at[z_peer(k)], dst_ref=dst.at[z],
            send_sem=z_send.at[s, k - 1], recv_sem=z_recv.at[s, k - 1],
            device_id=(y, z_peer(k) * nq + q), device_id_type=MESH)

    def z_own(s):
        src, dst = z_refs(s)
        return pltpu.make_async_copy(src.at[z], dst.at[z], local_sem.at[s, 0])

    def q_copy(s, k):
        _, src = z_refs(s)
        return pltpu.make_async_remote_copy(
            src_ref=src.at[:, q_peer(k)], dst_ref=q_dst(s, q),
            send_sem=q_send.at[s, k - 1], recv_sem=q_recv.at[s, k - 1],
            device_id=(y, z * nq + q_peer(k)), device_id_type=MESH)

    def q_own(s):
        _, src = z_refs(s)
        return pltpu.make_async_copy(src.at[:, q], q_dst(s, q), local_sem.at[s, 1])

    def y_copy(s, k, way):
        block = y_block(s, q_source(k), y)
        return pltpu.make_async_remote_copy(
            src_ref=block, dst_ref=block,
            send_sem=y_send.at[s, k, way], recv_sem=y_recv.at[s, k, way],
            device_id=(up if way == 0 else down, e), device_id_type=MESH)

    def f_copy(s, k):
        way = 0 if k < nq // 2 else 1
        block = y_block(s, q_source(k), down if way == 0 else up)
        return pltpu.make_async_remote_copy(
            src_ref=block, dst_ref=block,
            send_sem=f_send.at[s, k], recv_sem=f_recv.at[s, k],
            device_id=(up if way == 0 else down, e), device_id_type=MESH)

    def h_copy(k):
        return pltpu.make_async_remote_copy(
            src_ref=own_hot, dst_ref=all_hot.at[y],
            send_sem=h_send.at[k - 1], recv_sem=h_recv.at[k - 1],
            device_id=(lax.rem(y + k, ny), e), device_id_type=MESH)

    hot_own = pltpu.make_async_copy(own_hot, all_hot.at[y], local_sem.at[0, 2])
    hot_own.start()
    for k in range(1, ny):
        h_copy(k).start()
    z_order = sorted(range(1, nz), key=lambda k: -min(k, nz - k))
    for s in range(chunks + 1):
        z_own(s).start()
        for k in z_order:
            z_copy(s, k).start()

    def pass_on(s, k):
        way = 0 if k < nq // 2 else 1
        y_copy(s, k, way).wait_recv()
        f_copy(s, k).start()

    for s in range(chunks + 1):
        z_own(s).wait()
        for k in z_order:
            z_copy(s, k).wait_recv()
        q_own(s).start()
        for k in range(1, nq):
            q_copy(s, k).start()
        for k in range(nq):
            if k == 0:
                q_own(s).wait()
            else:
                q_copy(s, k).wait_recv()
            y_copy(s, k, 0).start()
            y_copy(s, k, 1).start()
            if s > 0:
                pass_on(s - 1, k)
    for k in range(nq):
        pass_on(chunks, k)

    hot_own.wait()
    for k in range(1, ny):
        h_copy(k).wait()
    for s in range(chunks + 1):
        for k in range(1, nz):
            z_copy(s, k).wait_send()
        for k in range(1, nq):
            q_copy(s, k).wait_send()
        for k in range(nq):
            y_copy(s, k, 0).wait_send()
            y_copy(s, k, 1).wait_send()
            y_copy(s, k, 1 if k < nq // 2 else 0).wait_recv()
            f_copy(s, k).wait()


def exchange(send, send_hot, own_hot, nz, nq):
    slots, _, _, pieces, width = send.shape
    hot_slots, hot_width = send_hot.shape[-2:]
    bf16 = jnp.bfloat16
    steps = slots + 1
    dma = pltpu.SemaphoreType.DMA

    def body(*refs):
        exchange_kernel(nz, nq, *refs)

    hbm = pl.BlockSpec(memory_space=pl.ANY)
    vmem = pl.BlockSpec(memory_space=pltpu.VMEM)
    return pl.pallas_call(
        body,
        out_shape=(
            jax.ShapeDtypeStruct((slots, 4, nq, nz, pieces, width), bf16),
            jax.ShapeDtypeStruct((nz, nq, 4, hot_slots, hot_width), bf16),
            jax.ShapeDtypeStruct((4,) + own_hot.shape, bf16),
        ),
        in_specs=[hbm, hbm, vmem],
        out_specs=(hbm, hbm, hbm),
        scratch_shapes=[
            pltpu.VMEM((slots, nz, nq, pieces, width), bf16),
            pltpu.VMEM((nz, nq, hot_slots, hot_width), bf16),
            dma((steps, nz - 1)),
            dma((steps, nz - 1)),
            dma((steps, nq - 1)),
            dma((steps, nq - 1)),
            dma((steps, 3)),
            dma((steps, nq, 2)),
            dma((steps, nq, 2)),
            dma((steps, nq)),
            dma((steps, nq)),
            dma((3,)),
            dma((3,)),
        ],
        compiler_params=pltpu.CompilerParams(
            collective_id=0, has_side_effects=True, vmem_limit_bytes=24 * 1024 * 1024
        ),
        cost_estimate=pl.CostEstimate(flops=0, bytes_accessed=300_000_000, transcendentals=0),
    )(send, send_hot, own_hot)


def on_device(tokens, cotangent, gate_scale, expert_index, hot_index, w_gate, w_up, w_down):
    tok_rows, feature_width = tokens.shape
    experts = lax.axis_size("expert")
    nq = 8 if experts == 64 else 2
    nz = experts // nq
    capacity = 3 * tok_rows // (2 * experts)
    hot_slots = 8
    hot_expert = hot_index[0]
    route_grad = (gate_scale[:, None] * cotangent.astype(jnp.float32)).astype(jnp.bfloat16)
    both = jnp.concatenate([tokens, route_grad], axis=1)
    is_hot = expert_index == hot_expert
    not_hot = jnp.logical_not(is_hot)
    owners = lax.broadcasted_iota(jnp.int32, (tok_rows, experts), 1)
    member = ((expert_index[:, None] == owners) & not_hot[:, None]).astype(jnp.int32)
    bucket_place = jnp.sum((jnp.cumsum(member, axis=0) - 1) * member, axis=1)
    slot_index = bucket_place * experts + expert_index
    slot_grid = lax.broadcasted_iota(jnp.int32, (experts * capacity, tok_rows), 0)
    cold_map = ((slot_grid == slot_index[None, :]) & not_hot[None, :]).astype(jnp.bfloat16)
    hot_place = jnp.cumsum(is_hot.astype(jnp.int32)) - 1
    hot_grid = lax.broadcasted_iota(jnp.int32, (hot_slots, tok_rows), 0)
    hot_map = ((hot_grid == hot_place[None, :]) & is_hot[None, :]).astype(jnp.bfloat16)
    send = route_rows(cold_map, both)
    own_hot = route_rows(hot_map, both)
    part = feature_width // experts
    hot_width = -(-2 * part // 128) * 128
    send_hot = jnp.concatenate(
        [
            own_hot[:, :feature_width].reshape(hot_slots, experts, part),
            own_hot[:, feature_width:].reshape(hot_slots, experts, part),
            jnp.zeros((hot_slots, experts, hot_width - 2 * part), jnp.bfloat16),
        ],
        axis=2,
    ).transpose(1, 0, 2)
    width = 2 * feature_width // PIECES
    got, got_hot, all_hot = exchange(
        send.reshape(capacity, nz, nq, PIECES, width),
        send_hot.reshape(nz, nq, hot_slots, hot_width),
        own_hot,
        nz,
        nq,
    )
    shadow_gate, shadow_up, shadow_down = (
        spread(w_gate[0], "expert", hot_expert),
        spread(w_up[0], "expert", hot_expert),
        spread(w_down[0], "expert", hot_expert),
    )
    rows = got.reshape(capacity * 4 * experts, 2 * feature_width)
    cold_tokens, cold_grads = rows[:, :feature_width], rows[:, feature_width:]
    hidden, gate_grad, up_grad = expert_terms(
        cold_tokens, cold_grads, w_gate[0], w_up[0], w_down[0]
    )
    grad_gate = column_sum(cold_tokens, gate_grad).astype(jnp.bfloat16)
    grad_up = column_sum(cold_tokens, up_grad).astype(jnp.bfloat16)
    grad_down = column_sum(hidden, cold_grads).astype(jnp.bfloat16)
    hot_rows = all_hot.reshape(4 * hot_slots, 2 * feature_width)
    hot_hidden, hot_gate_grad, hot_up_grad = expert_terms(
        hot_rows[:, :feature_width], hot_rows[:, feature_width:],
        shadow_gate, shadow_up, shadow_down,
    )
    hot_terms = lax.all_gather(
        jnp.concatenate([hot_gate_grad, hot_up_grad, hot_hidden], axis=1),
        "expert", axis=0, tiled=True,
    )
    ff = w_gate.shape[2]
    sums = column_sum(got_hot.reshape(experts * 4 * hot_slots, hot_width), hot_terms)
    hot_grads = jnp.stack(
        [sums[:part, :ff], sums[:part, ff : 2 * ff], sums[part : 2 * part, 2 * ff :]], axis=1
    ).astype(jnp.bfloat16)[None]
    return (grad_gate[None], grad_up[None], grad_down[None], hot_grads)


def solution(mesh):
    placed = (
        P(("dp", "expert"), None),
        P(("dp", "expert"), None),
        P(("dp", "expert")),
        P(("dp", "expert")),
        P(),
        P("expert", None, "dp"),
        P("expert", None, "dp"),
        P("expert", "dp", None),
    )
    return jax.shard_map(
        on_device,
        mesh=mesh,
        in_specs=placed,
        out_specs=(
            P("expert", None, "dp"),
            P("expert", None, "dp"),
            P("expert", "dp", None),
            P(None, "expert", None, "dp"),
        ),
        check_vma=False,
    )
```

```python
import jax
import jax.numpy as jnp
from jax import lax
from jax.experimental import pallas as pl
from jax.experimental.pallas import tpu as pltpu
from jax.sharding import PartitionSpec as P

CONTRACT_ROWS = (((0,), (0,)), ((), ()))
MESH = pl.DeviceIdType.MESH
PIECES = 8


def terms_of(pre_gate, pre_up, hidden_back):
    sigmoid_gate = jax.nn.sigmoid(pre_gate)
    activated = pre_gate * sigmoid_gate
    hidden = (activated * pre_up).astype(jnp.bfloat16)
    gate_grad = (
        hidden_back * pre_up * sigmoid_gate * (1.0 + pre_gate * (1.0 - sigmoid_gate))
    ).astype(jnp.bfloat16)
    up_grad = (hidden_back * activated).astype(jnp.bfloat16)
    return (hidden, gate_grad, up_grad)


def expert_terms(row_tokens, row_grads, gate_matrix, up_matrix, down_matrix):
    pre_gate = jnp.dot(row_tokens, gate_matrix, preferred_element_type=jnp.float32)
    pre_up = jnp.dot(row_tokens, up_matrix, preferred_element_type=jnp.float32)
    hidden_back = lax.dot_general(
        row_grads, down_matrix, (((1,), (1,)), ((), ())), preferred_element_type=jnp.float32
    )
    return terms_of(pre_gate, pre_up, hidden_back)


def column_sum(left, right):
    return lax.dot_general(left, right, CONTRACT_ROWS, preferred_element_type=jnp.float32)


def route_rows(selector, values):
    return jnp.dot(selector, values, preferred_element_type=jnp.float32).astype(jnp.bfloat16)


def exchange_kernel(nz, nx, nc, send, send_hot, hot_rows, hot_at, w_gate, w_up, w_down,
                    got, got_hot, hot_terms,
                    mid, mid_hot, pair_gu, pair_d, one_gu, one_d, row_gu, row_d,
                    two_gu, two_d, col_gu, col_d, three_gu, three_d, full_gu, full_d,
                    hot_in, part, parts, own_terms,
                    z_send, z_recv, q_send, q_recv, local_sem,
                    y_send, y_recv, f_send, f_recv,
                    c_send, c_recv, x_send, x_recv, w_send, w_recv, g_send, g_recv,
                    r_send, r_recv, v_send, v_recv, p_send, p_recv,
                    t_send, t_recv, u_send, u_recv, b_send, b_recv, own_sem):
    ny = 4
    nq = nx * nc
    chunks = send.shape[0]
    y = lax.axis_index("dp")
    e = lax.axis_index("expert")
    z = lax.div(e, nq)
    q = lax.rem(e, nq)
    x = lax.div(q, nc)
    c = lax.rem(q, nc)
    up = lax.rem(y + 1, ny)
    down = lax.rem(y + ny - 1, ny)
    twin = (y, z * nq + x * nc + (1 - c))
    half = w_gate.shape[0] // nc
    width = w_gate.shape[1]
    span = one_gu.shape[1] // 14 * 4
    z_rows = span // nz
    d_rows = width // nz

    def z_peer(k):
        return lax.rem(z + k, nz)

    def q_peer(k):
        return lax.rem(q + k, nq)

    def q_source(k):
        return lax.rem(q + nq - k, nq)

    def x_peer(k):
        return lax.rem(x + k, nx)

    def z_dev(k):
        return (y, z_peer(k) * nq + q)

    def q_dev(k):
        return (y, z * nq + q_peer(k))

    def x_dev(k):
        return (y, z * nq + x_peer(k) * nc + c)

    def remote(src, dst, send_sem, recv_sem, device):
        return pltpu.make_async_remote_copy(
            src_ref=src, dst_ref=dst, send_sem=send_sem, recv_sem=recv_sem,
            device_id=device, device_id_type=MESH)

    barrier = pltpu.get_barrier_semaphore()
    for k in range(1, nz):
        pl.semaphore_signal(barrier, inc=1, device_id=z_dev(k), device_id_type=MESH)
    for k in range(1, nq):
        pl.semaphore_signal(barrier, inc=1, device_id=q_dev(k), device_id_type=MESH)
    for k in range(1, ny):
        pl.semaphore_signal(barrier, inc=1, device_id=(lax.rem(y + k, ny), e), device_id_type=MESH)
    pl.semaphore_wait(barrier, nz - 1 + nq - 1 + ny - 1)

    def z_refs(s):
        if s < chunks:
            return send.at[s], mid.at[s]
        return send_hot, mid_hot

    def q_dst(s, who):
        if s < chunks:
            return got.at[s, y, who]
        return got_hot.at[:, who, y]

    def y_block(s, who, plane):
        if s < chunks:
            return got.at[s, plane, who]
        return got_hot.at[:, who, plane]

    def z_copy(s, k):
        src, dst = z_refs(s)
        return remote(src.at[z_peer(k)], dst.at[z], z_send.at[s, k - 1], z_recv.at[s, k - 1], z_dev(k))

    def z_own(s):
        src, dst = z_refs(s)
        return pltpu.make_async_copy(src.at[z], dst.at[z], local_sem.at[s, 0])

    def q_copy(s, k):
        _, src = z_refs(s)
        return remote(src.at[:, q_peer(k)], q_dst(s, q), q_send.at[s, k - 1], q_recv.at[s, k - 1], q_dev(k))

    def q_own(s):
        _, src = z_refs(s)
        return pltpu.make_async_copy(src.at[:, q], q_dst(s, q), local_sem.at[s, 1])

    def y_copy(s, k, way):
        block = y_block(s, q_source(k), y)
        return remote(block, block, y_send.at[s, k, way], y_recv.at[s, k, way],
                      (up if way == 0 else down, e))

    def f_copy(s, k):
        way = 0 if k < nq // 2 else 1
        block = y_block(s, q_source(k), down if way == 0 else up)
        return remote(block, block, f_send.at[s, k], f_recv.at[s, k],
                      (up if way == 0 else down, e))

    z_order = sorted(range(1, nz), key=lambda k: -min(k, nz - k))

    def start_z(s):
        z_own(s).start()
        for k in z_order:
            z_copy(s, k).start()

    def pass_on(s, k):
        way = 0 if k < nq // 2 else 1
        y_copy(s, k, way).wait_recv()
        f_copy(s, k).start()

    def run_chunk(s):
        z_own(s).wait()
        for k in z_order:
            z_copy(s, k).wait_recv()
        q_own(s).start()
        for k in range(1, nq):
            q_copy(s, k).start()
        for k in range(nq):
            if k == 0:
                q_own(s).wait()
            else:
                q_copy(s, k).wait_recv()
            y_copy(s, k, 0).start()
            y_copy(s, k, 1).start()
            if s > 0:
                pass_on(s - 1, k)

    def row_half(who):
        return pl.ds(pl.multiple_of(who * half, half), half)

    def c_copies(who):
        return (
            (w_gate.at[row_half(who), :], pair_gu.at[c, 0]),
            (w_up.at[row_half(who), :], pair_gu.at[c, 1]),
            (w_down.at[:, row_half(who)], pair_d.at[c]),
        )

    def c_copy(i):
        src, dst = c_copies(1 - c)[i]
        return remote(src, dst, c_send.at[i], c_recv.at[i], twin)

    def c_own(i):
        src, dst = c_copies(c)[i]
        return pltpu.make_async_copy(src, dst, own_sem.at[i])

    def x_span(who):
        first = who * 3 + lax.div(who, 2)
        return pl.ds(pl.multiple_of(first * (half // 14), half // 14), span)

    def x_pair(who):
        return (
            (one_gu.at[:, x_span(who), :], row_gu.at[x]),
            (one_d.at[:, x_span(who)], row_d.at[x]),
        )

    def x_copy(k, i):
        src, dst = x_pair(x_peer(k))[i]
        return remote(src, dst, x_send.at[k - 1, i], x_recv.at[k - 1, i], x_dev(k))

    def x_own(i):
        src, dst = x_pair(x)[i]
        return pltpu.make_async_copy(src, dst, own_sem.at[3 + i])

    def z_part(who):
        return pl.ds(pl.multiple_of(who * z_rows, z_rows), z_rows)

    def d_part(who):
        return pl.ds(pl.multiple_of(who * d_rows, d_rows), d_rows)

    def w_pair(who):
        return (
            (two_gu.at[:, z_part(who), :], col_gu.at[z]),
            (two_d.at[d_part(who), :], col_d.at[z]),
        )

    def w_copy(k, i):
        src, dst = w_pair(z_peer(k))[i]
        return remote(src, dst, w_send.at[k - 1, i], w_recv.at[k - 1, i], z_dev(k))

    def w_own(i):
        src, dst = w_pair(z)[i]
        return pltpu.make_async_copy(src, dst, own_sem.at[5 + i])

    g_pair = (
        (three_gu, full_gu.at[:, z_part(z), :]),
        (three_d, full_d.at[d_part(z), :]),
    )

    def g_copy(k, i):
        src, dst = g_pair[i]
        return remote(src, dst, g_send.at[k - 1, i], g_recv.at[k - 1, i], z_dev(k))

    def g_own(i):
        src, dst = g_pair[i]
        return pltpu.make_async_copy(src, dst, own_sem.at[7 + i])

    def r_copy(k):
        return remote(hot_rows.at[q_peer(k)], hot_in.at[y, q], r_send.at[k - 1], r_recv.at[k - 1], q_dev(k))

    r_own = pltpu.make_async_copy(hot_rows.at[q], hot_in.at[y, q], own_sem.at[9])

    def v_copy(k):
        return remote(hot_in.at[y], hot_in.at[y], v_send.at[k - 1], v_recv.at[k - 1],
                      (lax.rem(y + k, ny), e))

    def p_copy(k):
        return remote(part.at[:, q_peer(k)], parts.at[q], p_send.at[k - 1], p_recv.at[k - 1], q_dev(k))

    p_own = pltpu.make_async_copy(part.at[:, q], parts.at[q], own_sem.at[10])

    def t_copy(k):
        return remote(own_terms, hot_terms.at[z, x, c], t_send.at[k - 1], t_recv.at[k - 1], z_dev(k))

    t_own = pltpu.make_async_copy(own_terms, hot_terms.at[z, x, c], own_sem.at[11])

    def u_copy(k):
        block = hot_terms.at[:, x, c]
        return remote(block, block, u_send.at[k - 1], u_recv.at[k - 1], x_dev(k))

    def b_copy():
        block = hot_terms.at[:, :, c]
        return remote(block, block, b_send.at[0], b_recv.at[0], twin)

    hot_z = hot_at[0]
    hot_x = hot_at[1]
    hot_c = hot_at[2]

    for i in range(3):
        c_copy(i).start()
        c_own(i).start()
    r_own.start()
    for k in range(1, nq):
        r_copy(k).start()
    start_z(0)
    start_z(chunks)
    start_z(1)
    for i in range(3):
        c_own(i).wait()
        c_copy(i).wait_recv()

    tile = half // 14

    def keep_half(n, carry):
        rows = pl.ds(pl.multiple_of(n * tile, tile), tile)
        one_gu[0, rows, :] = pair_gu[hot_c, 0, rows, :]
        one_gu[1, rows, :] = pair_gu[hot_c, 1, rows, :]
        one_d[:, rows] = pair_d[hot_c, :, rows]
        return carry

    lax.fori_loop(0, 14, keep_half, 0)
    for i in range(2):
        x_own(i).start()
        for k in range(1, nx):
            x_copy(k, i).start()

    r_own.wait()
    for k in range(1, nq):
        r_copy(k).wait_recv()
    for k in range(1, ny):
        v_copy(k).start()

    run_chunk(0)

    for i in range(2):
        x_own(i).wait()
        for k in range(1, nx):
            x_copy(k, i).wait_recv()
    two_gu[...] = row_gu[hot_x]
    two_d[...] = row_d[hot_x]
    for i in range(2):
        w_own(i).start()
        for k in z_order:
            w_copy(k, i).start()
    start_z(2)

    run_chunk(1)

    for i in range(2):
        w_own(i).wait()
        for k in z_order:
            w_copy(k, i).wait_recv()
    three_gu[...] = col_gu[hot_z]
    three_d[...] = col_d[hot_z]
    for i in range(2):
        g_own(i).start()
        for k in z_order:
            g_copy(k, i).start()

    run_chunk(2)

    for k in range(1, ny):
        v_copy(k).wait_recv()
    for i in range(2):
        g_own(i).wait()
        for k in z_order:
            g_copy(k, i).wait_recv()
    rows = hot_in[...].astype(jnp.float32).reshape(ny * nq * 8, 2 * span).astype(jnp.bfloat16)
    row_tokens, row_grads = rows[:, :span], rows[:, span:]
    flat = (ny, nq, 8, width)
    part[:, :, :, 0:width] = jnp.dot(
        row_tokens, full_gu[0], preferred_element_type=jnp.float32).reshape(flat)
    part[:, :, :, width : 2 * width] = jnp.dot(
        row_tokens, full_gu[1], preferred_element_type=jnp.float32).reshape(flat)
    part[:, :, :, 2 * width :] = lax.dot_general(
        row_grads, full_d[...], (((1,), (1,)), ((), ())),
        preferred_element_type=jnp.float32).reshape(flat)
    p_own.start()
    for k in range(1, nq):
        p_copy(k).start()

    run_chunk(chunks)

    p_own.wait()
    for k in range(1, nq):
        p_copy(k).wait_recv()
    total = parts[0]
    for k in range(1, nq):
        total = total + parts[k]
    total = total.reshape(ny * 8, 3 * width)
    pre_gate, pre_up, hidden_back = (
        total[:, :width], total[:, width : 2 * width], total[:, 2 * width :])
    hidden, gate_grad, up_grad = terms_of(pre_gate, pre_up, hidden_back)
    own_terms[:, 0:width] = gate_grad
    own_terms[:, width : 2 * width] = up_grad
    own_terms[:, 2 * width :] = hidden
    t_own.start()
    for k in z_order:
        t_copy(k).start()

    for k in range(nq):
        pass_on(chunks, k)

    t_own.wait()
    for k in z_order:
        t_copy(k).wait_recv()
    for k in range(1, nx):
        u_copy(k).start()
    for k in range(1, nx):
        u_copy(k).wait_recv()
    b_copy().start()
    b_copy().wait()

    for i in range(3):
        c_copy(i).wait_send()
    for k in range(1, nx):
        u_copy(k).wait_send()
        for i in range(2):
            x_copy(k, i).wait_send()
    for k in range(1, nz):
        t_copy(k).wait_send()
        for i in range(2):
            w_copy(k, i).wait_send()
            g_copy(k, i).wait_send()
    for k in range(1, ny):
        v_copy(k).wait_send()
    for k in range(1, nq):
        r_copy(k).wait_send()
        p_copy(k).wait_send()
    for s in range(chunks + 1):
        for k in range(1, nz):
            z_copy(s, k).wait_send()
        for k in range(1, nq):
            q_copy(s, k).wait_send()
        for k in range(nq):
            y_copy(s, k, 0).wait_send()
            y_copy(s, k, 1).wait_send()
            y_copy(s, k, 1 if k < nq // 2 else 0).wait_recv()
            f_copy(s, k).wait()


def exchange(send, send_hot, hot_rows, hot_at, w_gate, w_up, w_down, nz, nx, nc):
    slots, _, nq, pieces, wide = send.shape
    hot_slots, hot_width = send_hot.shape[-2:]
    bf16, f32 = jnp.bfloat16, jnp.float32
    steps = slots + 1
    dma = pltpu.SemaphoreType.DMA
    rows, width = w_gate.shape
    half = rows // nc
    span = half // 14 * 4

    def body(*refs):
        exchange_kernel(nz, nx, nc, *refs)

    hbm = pl.BlockSpec(memory_space=pl.ANY)
    vmem = pl.BlockSpec(memory_space=pltpu.VMEM)
    smem = pl.BlockSpec(memory_space=pltpu.SMEM)
    return pl.pallas_call(
        body,
        out_shape=(
            jax.ShapeDtypeStruct((slots, 4, nq, nz, pieces, wide), bf16),
            jax.ShapeDtypeStruct((nz, nq, 4, hot_slots, hot_width), bf16),
            jax.ShapeDtypeStruct((nz, nx, nc, 4 * hot_slots, 3 * width), bf16),
        ),
        in_specs=[hbm, hbm, vmem, smem, hbm, hbm, hbm],
        out_specs=(hbm, hbm, hbm),
        scratch_shapes=[
            pltpu.VMEM((slots, nz, nq, pieces, wide), bf16),
            pltpu.VMEM((nz, nq, hot_slots, hot_width), bf16),
            pltpu.VMEM((nc, 2, half, width), bf16),
            pltpu.VMEM((nc, width, half), bf16),
            pltpu.VMEM((2, half, width), bf16),
            pltpu.VMEM((width, half), bf16),
            pltpu.VMEM((nx, 2, span, width), bf16),
            pltpu.VMEM((nx, width, span), bf16),
            pltpu.VMEM((2, span, width), bf16),
            pltpu.VMEM((width, span), bf16),
            pltpu.VMEM((nz, 2, span // nz, width), bf16),
            pltpu.VMEM((nz, width // nz, span), bf16),
            pltpu.VMEM((2, span // nz, width), bf16),
            pltpu.VMEM((width // nz, span), bf16),
            pltpu.VMEM((2, span, width), bf16),
            pltpu.VMEM((width, span), bf16),
            pltpu.VMEM((4, nq, hot_slots, 2 * span), bf16),
            pltpu.VMEM((4, nq, hot_slots, 3 * width), f32),
            pltpu.VMEM((nq, 4, hot_slots, 3 * width), f32),
            pltpu.VMEM((4 * hot_slots, 3 * width), bf16),
            dma((steps, nz - 1)),
            dma((steps, nz - 1)),
            dma((steps, nq - 1)),
            dma((steps, nq - 1)),
            dma((steps, 2)),
            dma((steps, nq, 2)),
            dma((steps, nq, 2)),
            dma((steps, nq)),
            dma((steps, nq)),
            dma((3,)),
            dma((3,)),
            dma((nx - 1, 2)),
            dma((nx - 1, 2)),
            dma((nz - 1, 2)),
            dma((nz - 1, 2)),
            dma((nz - 1, 2)),
            dma((nz - 1, 2)),
            dma((nq - 1,)),
            dma((nq - 1,)),
            dma((3,)),
            dma((3,)),
            dma((nq - 1,)),
            dma((nq - 1,)),
            dma((nz - 1,)),
            dma((nz - 1,)),
            dma((nx - 1,)),
            dma((nx - 1,)),
            dma((1,)),
            dma((1,)),
            dma((12,)),
        ],
        compiler_params=pltpu.CompilerParams(
            collective_id=0, has_side_effects=True, vmem_limit_bytes=40 * 1024 * 1024
        ),
        cost_estimate=pl.CostEstimate(flops=0, bytes_accessed=300_000_000, transcendentals=0),
    )(send, send_hot, hot_rows, hot_at, w_gate, w_up, w_down)


def on_device(tokens, cotangent, gate_scale, expert_index, hot_index, w_gate, w_up, w_down):
    tok_rows, feature_width = tokens.shape
    experts = lax.axis_size("expert")
    nx, nc = 4, 2
    nq = nx * nc
    nz = experts // nq
    capacity = 3 * tok_rows // (2 * experts)
    hot_slots = 8
    hot_expert = hot_index[0]
    route_grad = (gate_scale[:, None] * cotangent.astype(jnp.float32)).astype(jnp.bfloat16)
    both = jnp.concatenate([tokens, route_grad], axis=1)
    is_hot = expert_index == hot_expert
    not_hot = jnp.logical_not(is_hot)
    owners = lax.broadcasted_iota(jnp.int32, (tok_rows, experts), 1)
    member = ((expert_index[:, None] == owners) & not_hot[:, None]).astype(jnp.int32)
    bucket_place = jnp.sum((jnp.cumsum(member, axis=0) - 1) * member, axis=1)
    slot_index = bucket_place * experts + expert_index
    slot_grid = lax.broadcasted_iota(jnp.int32, (experts * capacity, tok_rows), 0)
    cold_map = ((slot_grid == slot_index[None, :]) & not_hot[None, :]).astype(jnp.bfloat16)
    hot_place = jnp.cumsum(is_hot.astype(jnp.int32)) - 1
    hot_grid = lax.broadcasted_iota(jnp.int32, (hot_slots, tok_rows), 0)
    hot_map = ((hot_grid == hot_place[None, :]) & is_hot[None, :]).astype(jnp.bfloat16)
    send = route_rows(cold_map, both)
    own_hot = route_rows(hot_map, both)
    part = feature_width // experts
    hot_width = -(-2 * part // 128) * 128
    send_hot = jnp.concatenate(
        [
            own_hot[:, :feature_width].reshape(hot_slots, experts, part),
            own_hot[:, feature_width:].reshape(hot_slots, experts, part),
            jnp.zeros((hot_slots, experts, hot_width - 2 * part), jnp.bfloat16),
        ],
        axis=2,
    ).transpose(1, 0, 2)
    width = 2 * feature_width // PIECES
    half = feature_width // nc
    tile = half // 14
    hot_rows = jnp.stack(
        [
            jnp.concatenate(
                [
                    jnp.concatenate(
                        [
                            own_hot[:, at : at + (3 + x % 2) * tile],
                            jnp.zeros((hot_slots, (1 - x % 2) * tile), jnp.bfloat16),
                        ],
                        axis=1,
                    )
                    for at in (
                        c * half + (7 * x // 2) * tile,
                        feature_width + c * half + (7 * x // 2) * tile,
                    )
                ],
                axis=1,
            )
            for x in range(nx)
            for c in range(nc)
        ]
    )
    hot_at = jnp.stack([hot_expert // nq, hot_expert % nq // nc, hot_expert % nc])
    got, got_hot, hot_terms = exchange(
        send.reshape(capacity, nz, nq, PIECES, width),
        send_hot.reshape(nz, nq, hot_slots, hot_width),
        hot_rows,
        hot_at,
        w_gate[0],
        w_up[0],
        w_down[0],
        nz,
        nx,
        nc,
    )
    rows = got.reshape(capacity * 4 * experts, 2 * feature_width)
    cold_tokens, cold_grads = rows[:, :feature_width], rows[:, feature_width:]
    hidden, gate_grad, up_grad = expert_terms(
        cold_tokens, cold_grads, w_gate[0], w_up[0], w_down[0]
    )
    grad_gate = column_sum(cold_tokens, gate_grad).astype(jnp.bfloat16)
    grad_up = column_sum(cold_tokens, up_grad).astype(jnp.bfloat16)
    grad_down = column_sum(hidden, cold_grads).astype(jnp.bfloat16)
    ff = w_gate.shape[2]
    hot_total = experts * 4 * hot_slots
    sums = column_sum(
        got_hot.reshape(hot_total, hot_width), hot_terms.reshape(hot_total, 3 * ff)
    )
    hot_grads = jnp.stack(
        [sums[:part, :ff], sums[:part, ff : 2 * ff], sums[part : 2 * part, 2 * ff :]], axis=1
    ).astype(jnp.bfloat16)[None]
    return (grad_gate[None], grad_up[None], grad_down[None], hot_grads)


def solution(mesh):
    placed = (
        P(("dp", "expert"), None),
        P(("dp", "expert"), None),
        P(("dp", "expert")),
        P(("dp", "expert")),
        P(),
        P("expert", None, "dp"),
        P("expert", None, "dp"),
        P("expert", "dp", None),
    )
    return jax.shard_map(
        on_device,
        mesh=mesh,
        in_specs=placed,
        out_specs=(
            P("expert", None, "dp"),
            P("expert", None, "dp"),
            P("expert", "dp", None),
            P(None, "expert", None, "dp"),
        ),
        check_vma=False,
    )
```

```python
import jax
import jax.numpy as jnp
from jax import lax
from jax.experimental import pallas as pl
from jax.experimental.pallas import tpu as pltpu
from jax.sharding import PartitionSpec as P

CONTRACT_ROWS = (((0,), (0,)), ((), ()))
MESH = pl.DeviceIdType.MESH
PIECES = 8


def terms_of(pre_gate, pre_up, hidden_back):
    sigmoid_gate = jax.nn.sigmoid(pre_gate)
    activated = pre_gate * sigmoid_gate
    hidden = (activated * pre_up).astype(jnp.bfloat16)
    gate_grad = (
        hidden_back * pre_up * sigmoid_gate * (1.0 + pre_gate * (1.0 - sigmoid_gate))
    ).astype(jnp.bfloat16)
    up_grad = (hidden_back * activated).astype(jnp.bfloat16)
    return (hidden, gate_grad, up_grad)


def column_sum(left, right):
    return lax.dot_general(left, right, CONTRACT_ROWS, preferred_element_type=jnp.float32)


def route_rows(selector, values):
    return jnp.dot(selector, values, preferred_element_type=jnp.float32).astype(jnp.bfloat16)


def exchange_kernel(nz, nx, nc, send, send_hot, hot_rows, hot_at, w_gate, w_up, w_down,
                    got, got_hot, hot_terms,
                    mid, mid_hot, turned, pair_gu, pair_d, one_gu, one_d, row_gu, row_d,
                    two_gu, two_d, col_gu, col_d, three_gu, three_d, full_gu, full_d,
                    hot_in, part, parts, own_terms,
                    z_send, z_recv, q_send, q_recv, local_sem,
                    y_send, y_recv, f_send, f_recv,
                    c_send, c_recv, x_send, x_recv, w_send, w_recv, g_send, g_recv,
                    r_send, r_recv, v_send, v_recv, p_send, p_recv,
                    t_send, t_recv, u_send, u_recv, b_send, b_recv, own_sem):
    ny = 4
    nq = nx * nc
    chunks = send.shape[0]
    pieces = send.shape[3]
    group = 4
    y = lax.axis_index("dp")
    e = lax.axis_index("expert")
    z = lax.div(e, nq)
    q = lax.rem(e, nq)
    x = lax.div(q, nc)
    c = lax.rem(q, nc)
    up = lax.rem(y + 1, ny)
    down = lax.rem(y + ny - 1, ny)
    twin = (y, z * nq + x * nc + (1 - c))
    half = w_gate.shape[0] // nc
    width = w_gate.shape[1]
    span = one_gu.shape[1] // 14 * 4
    z_rows = span // nz
    d_rows = width // nz

    def z_peer(k):
        return lax.rem(z + k, nz)

    def q_peer(k):
        return lax.rem(q + k, nq)

    def q_source(k):
        return lax.rem(q + nq - k, nq)

    def x_peer(k):
        return lax.rem(x + k, nx)

    def z_dev(k):
        return (y, z_peer(k) * nq + q)

    def q_dev(k):
        return (y, z * nq + q_peer(k))

    def x_dev(k):
        return (y, z * nq + x_peer(k) * nc + c)

    def remote(src, dst, send_sem, recv_sem, device):
        return pltpu.make_async_remote_copy(
            src_ref=src, dst_ref=dst, send_sem=send_sem, recv_sem=recv_sem,
            device_id=device, device_id_type=MESH)

    barrier = pltpu.get_barrier_semaphore()
    for k in range(1, nz):
        pl.semaphore_signal(barrier, inc=1, device_id=z_dev(k), device_id_type=MESH)
    for k in range(1, nq):
        pl.semaphore_signal(barrier, inc=1, device_id=q_dev(k), device_id_type=MESH)
    for k in range(1, ny):
        pl.semaphore_signal(barrier, inc=1, device_id=(lax.rem(y + k, ny), e), device_id_type=MESH)
    pl.semaphore_wait(barrier, nz - 1 + nq - 1 + ny - 1)

    def z_refs(s):
        if s < chunks:
            return send.at[s], mid.at[s]
        return send_hot, mid_hot

    def q_dst(s, who):
        if s < chunks:
            return got.at[:, (s * ny + y) * nq + who]
        return got_hot.at[:, who, y]

    def y_block(s, who, plane):
        if s < chunks:
            return got.at[:, (s * ny + plane) * nq + who]
        return got_hot.at[:, who, plane]

    def z_copy(s, k):
        src, dst = z_refs(s)
        return remote(src.at[z_peer(k)], dst.at[z], z_send.at[s, k - 1], z_recv.at[s, k - 1], z_dev(k))

    def z_own(s):
        src, dst = z_refs(s)
        return pltpu.make_async_copy(src.at[z], dst.at[z], local_sem.at[s, 0])

    def q_src(s, who):
        if s < chunks:
            return turned.at[s, who]
        return mid_hot.at[:, who]

    def q_copy(s, k):
        return remote(q_src(s, q_peer(k)), q_dst(s, q), q_send.at[s, k - 1], q_recv.at[s, k - 1], q_dev(k))

    def q_own(s):
        return pltpu.make_async_copy(q_src(s, q), q_dst(s, q), local_sem.at[s, 1])

    def y_copy(s, k, way):
        block = y_block(s, q_source(k), y)
        return remote(block, block, y_send.at[s, k, way], y_recv.at[s, k, way],
                      (up if way == 0 else down, e))

    def f_copy(s, k):
        way = 0 if k < nq // 2 else 1
        block = y_block(s, q_source(k), down if way == 0 else up)
        return remote(block, block, f_send.at[s, k], f_recv.at[s, k],
                      (up if way == 0 else down, e))

    z_order = sorted(range(1, nz), key=lambda k: -min(k, nz - k))

    def start_z(s):
        z_own(s).start()
        for k in z_order:
            z_copy(s, k).start()

    def pass_on(s, k):
        way = 0 if k < nq // 2 else 1
        y_copy(s, k, way).wait_recv()
        f_copy(s, k).start()

    block_rows = nz * group * pieces
    to_row = lax.broadcasted_iota(jnp.int32, (block_rows, block_rows), 0)
    from_row = lax.broadcasted_iota(jnp.int32, (block_rows, block_rows), 1)
    wanted = (
        (to_row % nz) * (group * pieces)
        + (to_row // (pieces * nz)) * pieces
        + (to_row // nz) % pieces
    )
    turn_map = jnp.where(from_row == wanted, 1.0, 0.0).astype(jnp.bfloat16)

    def turn(s):
        for g in range(nq // group):
            block = mid[s, :, g * group : (g + 1) * group].astype(jnp.float32)
            block = block.reshape(block_rows, block.shape[-1]).astype(jnp.bfloat16)
            moved = jnp.dot(turn_map, block, preferred_element_type=jnp.float32)
            turned[s, g * group : (g + 1) * group] = moved.reshape(
                group, pieces, nz, moved.shape[-1]).astype(jnp.bfloat16)

    def run_chunk(s, passing=True):
        z_own(s).wait()
        for k in z_order:
            z_copy(s, k).wait_recv()
        if s < chunks:
            turn(s)
        q_own(s).start()
        for k in range(1, nq):
            q_copy(s, k).start()
        for k in range(nq):
            if k == 0:
                q_own(s).wait()
            else:
                q_copy(s, k).wait_recv()
            y_copy(s, k, 0).start()
            y_copy(s, k, 1).start()
            if s > 0 and passing:
                pass_on(s - 1, k)

    def row_half(who):
        return pl.ds(pl.multiple_of(who * half, half), half)

    def c_copies(who):
        return (
            (w_gate.at[row_half(who), :], pair_gu.at[c, 0]),
            (w_up.at[row_half(who), :], pair_gu.at[c, 1]),
            (w_down.at[:, row_half(who)], pair_d.at[c]),
        )

    def c_copy(i):
        src, dst = c_copies(1 - c)[i]
        return remote(src, dst, c_send.at[i], c_recv.at[i], twin)

    def c_own(i):
        src, dst = c_copies(c)[i]
        return pltpu.make_async_copy(src, dst, own_sem.at[i])

    def x_span(who):
        first = who * 3 + lax.div(who, 2)
        return pl.ds(pl.multiple_of(first * (half // 14), half // 14), span)

    def x_pair(who):
        return (
            (one_gu.at[:, x_span(who), :], row_gu.at[x]),
            (one_d.at[:, x_span(who)], row_d.at[x]),
        )

    def x_copy(k, i):
        src, dst = x_pair(x_peer(k))[i]
        return remote(src, dst, x_send.at[k - 1, i], x_recv.at[k - 1, i], x_dev(k))

    def x_own(i):
        src, dst = x_pair(x)[i]
        return pltpu.make_async_copy(src, dst, own_sem.at[3 + i])

    def z_part(who):
        return pl.ds(pl.multiple_of(who * z_rows, z_rows), z_rows)

    def d_part(who):
        return pl.ds(pl.multiple_of(who * d_rows, d_rows), d_rows)

    def w_pair(who):
        return (
            (two_gu.at[:, z_part(who), :], col_gu.at[z]),
            (two_d.at[d_part(who), :], col_d.at[z]),
        )

    def w_copy(k, i):
        src, dst = w_pair(z_peer(k))[i]
        return remote(src, dst, w_send.at[k - 1, i], w_recv.at[k - 1, i], z_dev(k))

    def w_own(i):
        src, dst = w_pair(z)[i]
        return pltpu.make_async_copy(src, dst, own_sem.at[5 + i])

    g_pair = (
        (three_gu, full_gu.at[:, z_part(z), :]),
        (three_d, full_d.at[d_part(z), :]),
    )

    def g_copy(k, i):
        src, dst = g_pair[i]
        return remote(src, dst, g_send.at[k - 1, i], g_recv.at[k - 1, i], z_dev(k))

    def g_own(i):
        src, dst = g_pair[i]
        return pltpu.make_async_copy(src, dst, own_sem.at[7 + i])

    def r_copy(k):
        return remote(hot_rows.at[q_peer(k)], hot_in.at[y, q], r_send.at[k - 1], r_recv.at[k - 1], q_dev(k))

    r_own = pltpu.make_async_copy(hot_rows.at[q], hot_in.at[y, q], own_sem.at[9])

    def v_copy(k):
        return remote(hot_in.at[y], hot_in.at[y], v_send.at[k - 1], v_recv.at[k - 1],
                      (lax.rem(y + k, ny), e))

    def p_copy(k):
        return remote(part.at[:, q_peer(k)], parts.at[q], p_send.at[k - 1], p_recv.at[k - 1], q_dev(k))

    p_own = pltpu.make_async_copy(part.at[:, q], parts.at[q], own_sem.at[10])

    def t_copy(k):
        return remote(own_terms, hot_terms.at[z, x, c], t_send.at[k - 1], t_recv.at[k - 1], z_dev(k))

    t_own = pltpu.make_async_copy(own_terms, hot_terms.at[z, x, c], own_sem.at[11])

    def u_copy(k):
        block = hot_terms.at[:, x, c]
        return remote(block, block, u_send.at[k - 1], u_recv.at[k - 1], x_dev(k))

    def b_copy():
        block = hot_terms.at[:, :, c]
        return remote(block, block, b_send.at[0], b_recv.at[0], twin)

    hot_z = hot_at[0]
    hot_x = hot_at[1]
    hot_c = hot_at[2]

    for i in range(3):
        c_copy(i).start()
        c_own(i).start()
    r_own.start()
    for k in range(1, nq):
        r_copy(k).start()
    start_z(0)
    start_z(chunks)
    start_z(1)
    start_z(2)
    for i in range(3):
        c_own(i).wait()
        c_copy(i).wait_recv()

    tile = half // 14

    def keep_half(n, carry):
        rows = pl.ds(pl.multiple_of(n * tile, tile), tile)
        one_gu[0, rows, :] = pair_gu[hot_c, 0, rows, :]
        one_gu[1, rows, :] = pair_gu[hot_c, 1, rows, :]
        one_d[:, rows] = pair_d[hot_c, :, rows]
        return carry

    lax.fori_loop(0, 14, keep_half, 0)
    for i in range(2):
        x_own(i).start()
        for k in range(1, nx):
            x_copy(k, i).start()

    r_own.wait()
    for k in range(1, nq):
        r_copy(k).wait_recv()
    for k in range(1, ny):
        v_copy(k).start()

    run_chunk(0)

    for i in range(2):
        x_own(i).wait()
        for k in range(1, nx):
            x_copy(k, i).wait_recv()
    two_gu[...] = row_gu[hot_x]
    two_d[...] = row_d[hot_x]
    for i in range(2):
        w_own(i).start()
        for k in z_order:
            w_copy(k, i).start()

    run_chunk(1)

    for i in range(2):
        w_own(i).wait()
        for k in z_order:
            w_copy(k, i).wait_recv()
    three_gu[...] = col_gu[hot_z]
    three_d[...] = col_d[hot_z]
    for i in range(2):
        g_own(i).start()
        for k in z_order:
            g_copy(k, i).start()

    run_chunk(2)

    for k in range(1, ny):
        v_copy(k).wait_recv()
    for i in range(2):
        g_own(i).wait()
        for k in z_order:
            g_copy(k, i).wait_recv()
    rows = hot_in[...].astype(jnp.float32).reshape(ny * nq * 8, 2 * span).astype(jnp.bfloat16)
    row_tokens, row_grads = rows[:, :span], rows[:, span:]
    flat = (ny, nq, 8, width)
    part[:, :, :, 0:width] = jnp.dot(
        row_tokens, full_gu[0], preferred_element_type=jnp.float32).reshape(flat)
    part[:, :, :, width : 2 * width] = jnp.dot(
        row_tokens, full_gu[1], preferred_element_type=jnp.float32).reshape(flat)
    part[:, :, :, 2 * width :] = lax.dot_general(
        row_grads, full_d[...], (((1,), (1,)), ((), ())),
        preferred_element_type=jnp.float32).reshape(flat)
    p_own.start()
    for k in range(1, nq):
        p_copy(k).start()

    run_chunk(chunks, False)

    p_own.wait()
    for k in range(1, nq):
        p_copy(k).wait_recv()
    total = parts[0]
    for k in range(1, nq):
        total = total + parts[k]
    total = total.reshape(ny * 8, 3 * width)
    pre_gate, pre_up, hidden_back = (
        total[:, :width], total[:, width : 2 * width], total[:, 2 * width :])
    hidden, gate_grad, up_grad = terms_of(pre_gate, pre_up, hidden_back)
    own_terms[:, 0:width] = gate_grad
    own_terms[:, width : 2 * width] = up_grad
    own_terms[:, 2 * width :] = hidden
    t_own.start()
    for k in z_order:
        t_copy(k).start()

    for k in range(nq):
        pass_on(2, k)
    t_own.wait()
    for k in z_order:
        t_copy(k).wait_recv()
    for k in range(1, nx):
        u_copy(k).start()
    for k in range(nq):
        pass_on(chunks, k)
    for k in range(1, nx):
        u_copy(k).wait_recv()
    b_copy().start()
    b_copy().wait()

    for i in range(3):
        c_copy(i).wait_send()
    for k in range(1, nx):
        u_copy(k).wait_send()
        for i in range(2):
            x_copy(k, i).wait_send()
    for k in range(1, nz):
        t_copy(k).wait_send()
        for i in range(2):
            w_copy(k, i).wait_send()
            g_copy(k, i).wait_send()
    for k in range(1, ny):
        v_copy(k).wait_send()
    for k in range(1, nq):
        r_copy(k).wait_send()
        p_copy(k).wait_send()
    for s in range(chunks + 1):
        for k in range(1, nz):
            z_copy(s, k).wait_send()
        for k in range(1, nq):
            q_copy(s, k).wait_send()
        for k in range(nq):
            y_copy(s, k, 0).wait_send()
            y_copy(s, k, 1).wait_send()
            y_copy(s, k, 1 if k < nq // 2 else 0).wait_recv()
            f_copy(s, k).wait()


def exchange(send, send_hot, hot_rows, hot_at, w_gate, w_up, w_down, nz, nx, nc):
    slots, _, nq, pieces, wide = send.shape
    hot_slots, hot_width = send_hot.shape[-2:]
    bf16, f32 = jnp.bfloat16, jnp.float32
    steps = slots + 1
    dma = pltpu.SemaphoreType.DMA
    rows, width = w_gate.shape
    half = rows // nc
    span = half // 14 * 4

    def body(*refs):
        exchange_kernel(nz, nx, nc, *refs)

    hbm = pl.BlockSpec(memory_space=pl.ANY)
    vmem = pl.BlockSpec(memory_space=pltpu.VMEM)
    smem = pl.BlockSpec(memory_space=pltpu.SMEM)
    return pl.pallas_call(
        body,
        out_shape=(
            jax.ShapeDtypeStruct((pieces, slots * 4 * nq, nz, wide), bf16),
            jax.ShapeDtypeStruct((nz, nq, 4, hot_slots, hot_width), bf16),
            jax.ShapeDtypeStruct((nz, nx, nc, 4 * hot_slots, 3 * width), bf16),
        ),
        in_specs=[hbm, hbm, vmem, smem, hbm, hbm, hbm],
        out_specs=(hbm, hbm, hbm),
        scratch_shapes=[
            pltpu.VMEM((slots, nz, nq, pieces, wide), bf16),
            pltpu.VMEM((nz, nq, hot_slots, hot_width), bf16),
            pltpu.VMEM((slots, nq, pieces, nz, wide), bf16),
            pltpu.VMEM((nc, 2, half, width), bf16),
            pltpu.VMEM((nc, width, half), bf16),
            pltpu.VMEM((2, half, width), bf16),
            pltpu.VMEM((width, half), bf16),
            pltpu.VMEM((nx, 2, span, width), bf16),
            pltpu.VMEM((nx, width, span), bf16),
            pltpu.VMEM((2, span, width), bf16),
            pltpu.VMEM((width, span), bf16),
            pltpu.VMEM((nz, 2, span // nz, width), bf16),
            pltpu.VMEM((nz, width // nz, span), bf16),
            pltpu.VMEM((2, span // nz, width), bf16),
            pltpu.VMEM((width // nz, span), bf16),
            pltpu.VMEM((2, span, width), bf16),
            pltpu.VMEM((width, span), bf16),
            pltpu.VMEM((4, nq, hot_slots, 2 * span), bf16),
            pltpu.VMEM((4, nq, hot_slots, 3 * width), f32),
            pltpu.VMEM((nq, 4, hot_slots, 3 * width), f32),
            pltpu.VMEM((4 * hot_slots, 3 * width), bf16),
            dma((steps, nz - 1)),
            dma((steps, nz - 1)),
            dma((steps, nq - 1)),
            dma((steps, nq - 1)),
            dma((steps, 2)),
            dma((steps, nq, 2)),
            dma((steps, nq, 2)),
            dma((steps, nq)),
            dma((steps, nq)),
            dma((3,)),
            dma((3,)),
            dma((nx - 1, 2)),
            dma((nx - 1, 2)),
            dma((nz - 1, 2)),
            dma((nz - 1, 2)),
            dma((nz - 1, 2)),
            dma((nz - 1, 2)),
            dma((nq - 1,)),
            dma((nq - 1,)),
            dma((3,)),
            dma((3,)),
            dma((nq - 1,)),
            dma((nq - 1,)),
            dma((nz - 1,)),
            dma((nz - 1,)),
            dma((nx - 1,)),
            dma((nx - 1,)),
            dma((1,)),
            dma((1,)),
            dma((12,)),
        ],
        compiler_params=pltpu.CompilerParams(
            collective_id=0, has_side_effects=True, vmem_limit_bytes=40 * 1024 * 1024
        ),
        cost_estimate=pl.CostEstimate(flops=0, bytes_accessed=300_000_000, transcendentals=0),
    )(send, send_hot, hot_rows, hot_at, w_gate, w_up, w_down)


def on_device(tokens, cotangent, gate_scale, expert_index, hot_index, w_gate, w_up, w_down):
    tok_rows, feature_width = tokens.shape
    experts = lax.axis_size("expert")
    nx, nc = 4, 2
    nq = nx * nc
    nz = experts // nq
    capacity = 3 * tok_rows // (2 * experts)
    hot_slots = 8
    hot_expert = hot_index[0]
    route_grad = (gate_scale[:, None] * cotangent.astype(jnp.float32)).astype(jnp.bfloat16)
    both = jnp.concatenate([tokens, route_grad], axis=1)
    is_hot = expert_index == hot_expert
    not_hot = jnp.logical_not(is_hot)
    owners = lax.broadcasted_iota(jnp.int32, (tok_rows, experts), 1)
    member = ((expert_index[:, None] == owners) & not_hot[:, None]).astype(jnp.int32)
    bucket_place = jnp.sum((jnp.cumsum(member, axis=0) - 1) * member, axis=1)
    slot_index = bucket_place * experts + expert_index
    slot_grid = lax.broadcasted_iota(jnp.int32, (experts * capacity, tok_rows), 0)
    cold_map = ((slot_grid == slot_index[None, :]) & not_hot[None, :]).astype(jnp.bfloat16)
    hot_place = jnp.cumsum(is_hot.astype(jnp.int32)) - 1
    hot_grid = lax.broadcasted_iota(jnp.int32, (hot_slots, tok_rows), 0)
    hot_map = ((hot_grid == hot_place[None, :]) & is_hot[None, :]).astype(jnp.bfloat16)
    send = route_rows(cold_map, both)
    own_hot = route_rows(hot_map, both)
    part = feature_width // experts
    hot_width = -(-2 * part // 128) * 128
    send_hot = jnp.concatenate(
        [
            own_hot[:, :feature_width].reshape(hot_slots, experts, part),
            own_hot[:, feature_width:].reshape(hot_slots, experts, part),
            jnp.zeros((hot_slots, experts, hot_width - 2 * part), jnp.bfloat16),
        ],
        axis=2,
    ).transpose(1, 0, 2)
    width = 2 * feature_width // PIECES
    half = feature_width // nc
    tile = half // 14
    hot_rows = jnp.stack(
        [
            jnp.concatenate(
                [
                    jnp.concatenate(
                        [
                            own_hot[:, at : at + (3 + x % 2) * tile],
                            jnp.zeros((hot_slots, (1 - x % 2) * tile), jnp.bfloat16),
                        ],
                        axis=1,
                    )
                    for at in (
                        c * half + (7 * x // 2) * tile,
                        feature_width + c * half + (7 * x // 2) * tile,
                    )
                ],
                axis=1,
            )
            for x in range(nx)
            for c in range(nc)
        ]
    )
    hot_at = jnp.stack([hot_expert // nq, hot_expert % nq // nc, hot_expert % nc])
    got, got_hot, hot_terms = exchange(
        send.reshape(capacity, nz, nq, PIECES, width),
        send_hot.reshape(nz, nq, hot_slots, hot_width),
        hot_rows,
        hot_at,
        w_gate[0],
        w_up[0],
        w_down[0],
        nz,
        nx,
        nc,
    )
    rows = got.reshape(PIECES, capacity * 4 * experts, width)
    cold_tokens, cold_grads = rows[: PIECES // 2], rows[PIECES // 2 :]
    f32 = jnp.float32
    pre_gate = sum(
        jnp.dot(cold_tokens[n], w_gate[0, n * width : (n + 1) * width], preferred_element_type=f32)
        for n in range(PIECES // 2)
    )
    pre_up = sum(
        jnp.dot(cold_tokens[n], w_up[0, n * width : (n + 1) * width], preferred_element_type=f32)
        for n in range(PIECES // 2)
    )
    hidden_back = sum(
        lax.dot_general(
            cold_grads[n],
            w_down[0, :, n * width : (n + 1) * width],
            (((1,), (1,)), ((), ())),
            preferred_element_type=f32,
        )
        for n in range(PIECES // 2)
    )
    hidden, gate_grad, up_grad = terms_of(pre_gate, pre_up, hidden_back)
    grad_gate = lax.dot_general(
        cold_tokens, gate_grad, (((1,), (0,)), ((), ())), preferred_element_type=f32
    ).astype(jnp.bfloat16).reshape(feature_width, -1)
    grad_up = lax.dot_general(
        cold_tokens, up_grad, (((1,), (0,)), ((), ())), preferred_element_type=f32
    ).astype(jnp.bfloat16).reshape(feature_width, -1)
    grad_down = jnp.concatenate(
        [column_sum(hidden, cold_grads[n]).astype(jnp.bfloat16) for n in range(PIECES // 2)],
        axis=1,
    )
    ff = w_gate.shape[2]
    hot_total = experts * 4 * hot_slots
    sums = column_sum(
        got_hot.reshape(hot_total, hot_width), hot_terms.reshape(hot_total, 3 * ff)
    )
    hot_grads = jnp.stack(
        [sums[:part, :ff], sums[:part, ff : 2 * ff], sums[part : 2 * part, 2 * ff :]], axis=1
    ).astype(jnp.bfloat16)[None]
    return (grad_gate[None], grad_up[None], grad_down[None], hot_grads)


def solution(mesh):
    placed = (
        P(("dp", "expert"), None),
        P(("dp", "expert"), None),
        P(("dp", "expert")),
        P(("dp", "expert")),
        P(),
        P("expert", None, "dp"),
        P("expert", None, "dp"),
        P("expert", "dp", None),
    )
    return jax.shard_map(
        on_device,
        mesh=mesh,
        in_specs=placed,
        out_specs=(
            P("expert", None, "dp"),
            P("expert", None, "dp"),
            P("expert", "dp", None),
            P(None, "expert", None, "dp"),
        ),
        check_vma=False,
    )
```

```python
import jax
import jax.numpy as jnp
from jax import lax
from jax.experimental import pallas as pl
from jax.experimental.pallas import tpu as pltpu
from jax.sharding import PartitionSpec as P

CONTRACT_ROWS = (((0,), (0,)), ((), ()))
MESH = pl.DeviceIdType.MESH
PIECES = 8


def terms_of(pre_gate, pre_up, hidden_back):
    sigmoid_gate = jax.nn.sigmoid(pre_gate)
    activated = pre_gate * sigmoid_gate
    hidden = (activated * pre_up).astype(jnp.bfloat16)
    gate_grad = (
        hidden_back * pre_up * sigmoid_gate * (1.0 + pre_gate * (1.0 - sigmoid_gate))
    ).astype(jnp.bfloat16)
    up_grad = (hidden_back * activated).astype(jnp.bfloat16)
    return (hidden, gate_grad, up_grad)


def column_sum(left, right):
    return lax.dot_general(left, right, CONTRACT_ROWS, preferred_element_type=jnp.float32)


def route_rows(selector, values):
    return jnp.dot(selector, values, preferred_element_type=jnp.float32).astype(jnp.bfloat16)


def exchange_kernel(nz, nx, nc, send, send_hot, hot_rows, hot_at, w_gate, w_up, w_down,
                    got, got_hot, hot_terms, cold_hidden, cold_gate, cold_up,
                    mid, mid_hot, turned, pair_gu, pair_d, one_gu, one_d, row_gu, row_d,
                    two_gu, two_d, col_gu, col_d, three_gu, three_d, full_gu, full_d,
                    hot_in, part, parts, own_terms,
                    gate_here, up_here, down_here, slot_rows, sums,
                    z_send, z_recv, q_send, q_recv, local_sem,
                    y_send, y_recv, f_send, f_recv,
                    c_send, c_recv, x_send, x_recv, w_send, w_recv, g_send, g_recv,
                    r_send, r_recv, v_send, v_recv, p_send, p_recv,
                    t_send, t_recv, u_send, u_recv, b_send, b_recv, own_sem):
    ny = 4
    nq = nx * nc
    chunks = send.shape[0]
    pieces = send.shape[3]
    group = 4
    y = lax.axis_index("dp")
    e = lax.axis_index("expert")
    z = lax.div(e, nq)
    q = lax.rem(e, nq)
    x = lax.div(q, nc)
    c = lax.rem(q, nc)
    up = lax.rem(y + 1, ny)
    down = lax.rem(y + ny - 1, ny)
    twin = (y, z * nq + x * nc + (1 - c))
    half = w_gate.shape[0] // nc
    width = w_gate.shape[1]
    span = one_gu.shape[1] // 14 * 4
    z_rows = span // nz
    d_rows = width // nz

    def z_peer(k):
        return lax.rem(z + k, nz)

    def q_peer(k):
        return lax.rem(q + k, nq)

    def q_source(k):
        return lax.rem(q + nq - k, nq)

    def x_peer(k):
        return lax.rem(x + k, nx)

    def z_dev(k):
        return (y, z_peer(k) * nq + q)

    def q_dev(k):
        return (y, z * nq + q_peer(k))

    def x_dev(k):
        return (y, z * nq + x_peer(k) * nc + c)

    def remote(src, dst, send_sem, recv_sem, device):
        return pltpu.make_async_remote_copy(
            src_ref=src, dst_ref=dst, send_sem=send_sem, recv_sem=recv_sem,
            device_id=device, device_id_type=MESH)

    barrier = pltpu.get_barrier_semaphore()
    for k in range(1, nz):
        pl.semaphore_signal(barrier, inc=1, device_id=z_dev(k), device_id_type=MESH)
    for k in range(1, nq):
        pl.semaphore_signal(barrier, inc=1, device_id=q_dev(k), device_id_type=MESH)
    for k in range(1, ny):
        pl.semaphore_signal(barrier, inc=1, device_id=(lax.rem(y + k, ny), e), device_id_type=MESH)
    pl.semaphore_wait(barrier, nz - 1 + nq - 1 + ny - 1)

    def z_refs(s):
        if s < chunks:
            return send.at[s], mid.at[s]
        return send_hot, mid_hot

    def q_dst(s, who):
        if s < chunks:
            return got.at[:, (s * ny + y) * nq + who]
        return got_hot.at[:, who, y]

    def y_block(s, who, plane):
        if s < chunks:
            return got.at[:, (s * ny + plane) * nq + who]
        return got_hot.at[:, who, plane]

    def z_copy(s, k):
        src, dst = z_refs(s)
        return remote(src.at[z_peer(k)], dst.at[z], z_send.at[s, k - 1], z_recv.at[s, k - 1], z_dev(k))

    def z_own(s):
        src, dst = z_refs(s)
        return pltpu.make_async_copy(src.at[z], dst.at[z], local_sem.at[s, 0])

    def q_src(s, who):
        if s < chunks:
            return turned.at[s, who]
        return mid_hot.at[:, who]

    def q_copy(s, k):
        return remote(q_src(s, q_peer(k)), q_dst(s, q), q_send.at[s, k - 1], q_recv.at[s, k - 1], q_dev(k))

    def q_own(s):
        return pltpu.make_async_copy(q_src(s, q), q_dst(s, q), local_sem.at[s, 1])

    def y_copy(s, k, way):
        block = y_block(s, q_source(k), y)
        return remote(block, block, y_send.at[s, k, way], y_recv.at[s, k, way],
                      (up if way == 0 else down, e))

    def f_copy(s, k):
        way = 0 if k < nq // 2 else 1
        block = y_block(s, q_source(k), down if way == 0 else up)
        return remote(block, block, f_send.at[s, k], f_recv.at[s, k],
                      (up if way == 0 else down, e))

    z_order = sorted(range(1, nz), key=lambda k: -min(k, nz - k))

    def start_z(s):
        z_own(s).start()
        for k in z_order:
            z_copy(s, k).start()

    def pass_on(s, k):
        way = 0 if k < nq // 2 else 1
        y_copy(s, k, way).wait_recv()
        f_copy(s, k).start()

    block_rows = nz * group * pieces
    to_row = lax.broadcasted_iota(jnp.int32, (block_rows, block_rows), 0)
    from_row = lax.broadcasted_iota(jnp.int32, (block_rows, block_rows), 1)
    wanted = (
        (to_row % nz) * (group * pieces)
        + (to_row // (pieces * nz)) * pieces
        + (to_row // nz) % pieces
    )
    turn_map = jnp.where(from_row == wanted, 1.0, 0.0).astype(jnp.bfloat16)

    def turn(s):
        for g in range(nq // group):
            block = mid[s, :, g * group : (g + 1) * group].astype(jnp.float32)
            block = block.reshape(block_rows, block.shape[-1]).astype(jnp.bfloat16)
            moved = jnp.dot(turn_map, block, preferred_element_type=jnp.float32)
            turned[s, g * group : (g + 1) * group] = moved.reshape(
                group, pieces, nz, moved.shape[-1]).astype(jnp.bfloat16)

    def run_chunk(s, passing=True):
        z_own(s).wait()
        for k in z_order:
            z_copy(s, k).wait_recv()
        if s < chunks:
            turn(s)
        q_own(s).start()
        for k in range(1, nq):
            q_copy(s, k).start()
        for k in range(nq):
            if k == 0:
                q_own(s).wait()
            else:
                q_copy(s, k).wait_recv()
            y_copy(s, k, 0).start()
            y_copy(s, k, 1).start()
            if s > 0 and passing:
                pass_on(s - 1, k)

    def row_half(who):
        return pl.ds(pl.multiple_of(who * half, half), half)

    def c_copies(who):
        return (
            (w_gate.at[row_half(who), :], pair_gu.at[c, 0]),
            (w_up.at[row_half(who), :], pair_gu.at[c, 1]),
            (w_down.at[:, row_half(who)], pair_d.at[c]),
        )

    def c_copy(i):
        src, dst = c_copies(1 - c)[i]
        return remote(src, dst, c_send.at[i], c_recv.at[i], twin)

    def c_own(i):
        src, dst = c_copies(c)[i]
        return pltpu.make_async_copy(src, dst, own_sem.at[i])

    def x_span(who):
        first = who * 3 + lax.div(who, 2)
        return pl.ds(pl.multiple_of(first * (half // 14), half // 14), span)

    def x_pair(who):
        return (
            (one_gu.at[:, x_span(who), :], row_gu.at[x]),
            (one_d.at[:, x_span(who)], row_d.at[x]),
        )

    def x_copy(k, i):
        src, dst = x_pair(x_peer(k))[i]
        return remote(src, dst, x_send.at[k - 1, i], x_recv.at[k - 1, i], x_dev(k))

    def x_own(i):
        src, dst = x_pair(x)[i]
        return pltpu.make_async_copy(src, dst, own_sem.at[3 + i])

    def z_part(who):
        return pl.ds(pl.multiple_of(who * z_rows, z_rows), z_rows)

    def d_part(who):
        return pl.ds(pl.multiple_of(who * d_rows, d_rows), d_rows)

    def w_pair(who):
        return (
            (two_gu.at[:, z_part(who), :], col_gu.at[z]),
            (two_d.at[d_part(who), :], col_d.at[z]),
        )

    def w_copy(k, i):
        src, dst = w_pair(z_peer(k))[i]
        return remote(src, dst, w_send.at[k - 1, i], w_recv.at[k - 1, i], z_dev(k))

    def w_own(i):
        src, dst = w_pair(z)[i]
        return pltpu.make_async_copy(src, dst, own_sem.at[5 + i])

    g_pair = (
        (three_gu, full_gu.at[:, z_part(z), :]),
        (three_d, full_d.at[d_part(z), :]),
    )

    def g_copy(k, i):
        src, dst = g_pair[i]
        return remote(src, dst, g_send.at[k - 1, i], g_recv.at[k - 1, i], z_dev(k))

    def g_own(i):
        src, dst = g_pair[i]
        return pltpu.make_async_copy(src, dst, own_sem.at[7 + i])

    def r_copy(k):
        return remote(hot_rows.at[q_peer(k)], hot_in.at[y, q], r_send.at[k - 1], r_recv.at[k - 1], q_dev(k))

    r_own = pltpu.make_async_copy(hot_rows.at[q], hot_in.at[y, q], own_sem.at[9])

    def v_copy(k):
        return remote(hot_in.at[y], hot_in.at[y], v_send.at[k - 1], v_recv.at[k - 1],
                      (lax.rem(y + k, ny), e))

    def p_copy(k):
        return remote(part.at[:, q_peer(k)], parts.at[q], p_send.at[k - 1], p_recv.at[k - 1], q_dev(k))

    p_own = pltpu.make_async_copy(part.at[:, q], parts.at[q], own_sem.at[10])

    def t_copy(k):
        return remote(own_terms, hot_terms.at[z, x, c], t_send.at[k - 1], t_recv.at[k - 1], z_dev(k))

    t_own = pltpu.make_async_copy(own_terms, hot_terms.at[z, x, c], own_sem.at[11])

    def u_copy(k):
        block = hot_terms.at[:, x, c]
        return remote(block, block, u_send.at[k - 1], u_recv.at[k - 1], x_dev(k))

    def b_copy():
        block = hot_terms.at[:, :, c]
        return remote(block, block, b_send.at[0], b_recv.at[0], twin)

    here = ((w_gate, gate_here), (w_up, up_here), (w_down, down_here))

    def here_copy(i):
        return pltpu.make_async_copy(here[i][0], here[i][1], own_sem.at[12 + i])

    def cold(s):
        for k in range(nq):
            y_copy(s, k, 1 if k < nq // 2 else 0).wait_recv()
            f_copy(s, k).wait_recv()
        tiles = ny * nq
        taken = pltpu.make_async_copy(
            got.at[:, s * tiles : (s + 1) * tiles], slot_rows, own_sem.at[15])
        taken.start()
        taken.wait()
        step = slot_rows.shape[-1]
        count = tiles * nz

        def piece(n):
            block = slot_rows[n].astype(jnp.float32)
            return block.reshape(count, step).astype(jnp.bfloat16)

        for n in range(pieces // 2):
            cut = slice(n * step, (n + 1) * step)
            row_tokens, row_grads = piece(n), piece(pieces // 2 + n)
            new = (
                jnp.dot(row_tokens, gate_here[cut, :], preferred_element_type=jnp.float32),
                jnp.dot(row_tokens, up_here[cut, :], preferred_element_type=jnp.float32),
                lax.dot_general(row_grads, down_here[:, cut], (((1,), (1,)), ((), ())),
                                preferred_element_type=jnp.float32),
            )
            for m in range(3):
                if n == 0:
                    sums[m] = new[m]
                else:
                    sums[m] += new[m]
        hidden, gate_grad, up_grad = terms_of(sums[0], sums[1], sums[2])
        at = slice(s * count, (s + 1) * count)
        cold_hidden[at, :] = hidden
        cold_gate[at, :] = gate_grad
        cold_up[at, :] = up_grad

    hot_z = hot_at[0]
    hot_x = hot_at[1]
    hot_c = hot_at[2]

    for i in range(3):
        c_copy(i).start()
        c_own(i).start()
    r_own.start()
    for k in range(1, nq):
        r_copy(k).start()
    start_z(0)
    start_z(chunks)
    start_z(1)
    start_z(2)
    for i in range(3):
        c_own(i).wait()
        c_copy(i).wait_recv()

    for i in range(3):
        here_copy(i).start()
    tile = half // 14

    def keep_half(n, carry):
        rows = pl.ds(pl.multiple_of(n * tile, tile), tile)
        one_gu[0, rows, :] = pair_gu[hot_c, 0, rows, :]
        one_gu[1, rows, :] = pair_gu[hot_c, 1, rows, :]
        one_d[:, rows] = pair_d[hot_c, :, rows]
        return carry

    lax.fori_loop(0, 14, keep_half, 0)
    for i in range(2):
        x_own(i).start()
        for k in range(1, nx):
            x_copy(k, i).start()

    r_own.wait()
    for k in range(1, nq):
        r_copy(k).wait_recv()
    for k in range(1, ny):
        v_copy(k).start()

    run_chunk(0)

    for i in range(2):
        x_own(i).wait()
        for k in range(1, nx):
            x_copy(k, i).wait_recv()
    two_gu[...] = row_gu[hot_x]
    two_d[...] = row_d[hot_x]
    for i in range(2):
        w_own(i).start()
        for k in z_order:
            w_copy(k, i).start()

    run_chunk(1)

    for i in range(2):
        w_own(i).wait()
        for k in z_order:
            w_copy(k, i).wait_recv()
    three_gu[...] = col_gu[hot_z]
    three_d[...] = col_d[hot_z]
    for i in range(2):
        g_own(i).start()
        for k in z_order:
            g_copy(k, i).start()

    run_chunk(2)

    for k in range(1, ny):
        v_copy(k).wait_recv()
    for i in range(2):
        g_own(i).wait()
        for k in z_order:
            g_copy(k, i).wait_recv()
    rows = hot_in[...].astype(jnp.float32).reshape(ny * nq * 8, 2 * span).astype(jnp.bfloat16)
    row_tokens, row_grads = rows[:, :span], rows[:, span:]
    flat = (ny, nq, 8, width)
    part[:, :, :, 0:width] = jnp.dot(
        row_tokens, full_gu[0], preferred_element_type=jnp.float32).reshape(flat)
    part[:, :, :, width : 2 * width] = jnp.dot(
        row_tokens, full_gu[1], preferred_element_type=jnp.float32).reshape(flat)
    part[:, :, :, 2 * width :] = lax.dot_general(
        row_grads, full_d[...], (((1,), (1,)), ((), ())),
        preferred_element_type=jnp.float32).reshape(flat)
    p_own.start()
    for k in range(1, nq):
        p_copy(k).start()

    run_chunk(chunks, False)

    p_own.wait()
    for k in range(1, nq):
        p_copy(k).wait_recv()
    total = parts[0]
    for k in range(1, nq):
        total = total + parts[k]
    total = total.reshape(ny * 8, 3 * width)
    pre_gate, pre_up, hidden_back = (
        total[:, :width], total[:, width : 2 * width], total[:, 2 * width :])
    hidden, gate_grad, up_grad = terms_of(pre_gate, pre_up, hidden_back)
    own_terms[:, 0:width] = gate_grad
    own_terms[:, width : 2 * width] = up_grad
    own_terms[:, 2 * width :] = hidden
    t_own.start()
    for k in z_order:
        t_copy(k).start()

    for k in range(nq):
        pass_on(2, k)
    t_own.wait()
    for k in z_order:
        t_copy(k).wait_recv()
    for k in range(1, nx):
        u_copy(k).start()
    for k in range(nq):
        pass_on(chunks, k)
    for i in range(3):
        here_copy(i).wait()
    cold(0)
    cold(1)
    for k in range(1, nx):
        u_copy(k).wait_recv()
    b_copy().start()
    cold(2)
    b_copy().wait()

    for i in range(3):
        c_copy(i).wait_send()
    for k in range(1, nx):
        u_copy(k).wait_send()
        for i in range(2):
            x_copy(k, i).wait_send()
    for k in range(1, nz):
        t_copy(k).wait_send()
        for i in range(2):
            w_copy(k, i).wait_send()
            g_copy(k, i).wait_send()
    for k in range(1, ny):
        v_copy(k).wait_send()
    for k in range(1, nq):
        r_copy(k).wait_send()
        p_copy(k).wait_send()
    for s in range(chunks + 1):
        for k in range(1, nz):
            z_copy(s, k).wait_send()
        for k in range(1, nq):
            q_copy(s, k).wait_send()
        for k in range(nq):
            y_copy(s, k, 0).wait_send()
            y_copy(s, k, 1).wait_send()
            f_copy(s, k).wait_send()
            if s == chunks:
                y_copy(s, k, 1 if k < nq // 2 else 0).wait_recv()
                f_copy(s, k).wait_recv()


def exchange(send, send_hot, hot_rows, hot_at, w_gate, w_up, w_down, nz, nx, nc):
    slots, _, nq, pieces, wide = send.shape
    hot_slots, hot_width = send_hot.shape[-2:]
    bf16, f32 = jnp.bfloat16, jnp.float32
    steps = slots + 1
    dma = pltpu.SemaphoreType.DMA
    rows, width = w_gate.shape
    half = rows // nc
    span = half // 14 * 4

    def body(*refs):
        exchange_kernel(nz, nx, nc, *refs)

    hbm = pl.BlockSpec(memory_space=pl.ANY)
    vmem = pl.BlockSpec(memory_space=pltpu.VMEM)
    smem = pl.BlockSpec(memory_space=pltpu.SMEM)
    return pl.pallas_call(
        body,
        out_shape=(
            jax.ShapeDtypeStruct((pieces, slots * 4 * nq, nz, wide), bf16),
            jax.ShapeDtypeStruct((nz, nq, 4, hot_slots, hot_width), bf16),
            jax.ShapeDtypeStruct((nz, nx, nc, 4 * hot_slots, 3 * width), bf16),
            jax.ShapeDtypeStruct((slots * 4 * nq * nz, width), bf16),
            jax.ShapeDtypeStruct((slots * 4 * nq * nz, width), bf16),
            jax.ShapeDtypeStruct((slots * 4 * nq * nz, width), bf16),
        ),
        in_specs=[hbm, hbm, vmem, smem, hbm, hbm, hbm],
        out_specs=(hbm, hbm, hbm, vmem, vmem, vmem),
        scratch_shapes=[
            pltpu.VMEM((slots, nz, nq, pieces, wide), bf16),
            pltpu.VMEM((nz, nq, hot_slots, hot_width), bf16),
            pltpu.VMEM((slots, nq, pieces, nz, wide), bf16),
            pltpu.VMEM((nc, 2, half, width), bf16),
            pltpu.VMEM((nc, width, half), bf16),
            pltpu.VMEM((2, half, width), bf16),
            pltpu.VMEM((width, half), bf16),
            pltpu.VMEM((nx, 2, span, width), bf16),
            pltpu.VMEM((nx, width, span), bf16),
            pltpu.VMEM((2, span, width), bf16),
            pltpu.VMEM((width, span), bf16),
            pltpu.VMEM((nz, 2, span // nz, width), bf16),
            pltpu.VMEM((nz, width // nz, span), bf16),
            pltpu.VMEM((2, span // nz, width), bf16),
            pltpu.VMEM((width // nz, span), bf16),
            pltpu.VMEM((2, span, width), bf16),
            pltpu.VMEM((width, span), bf16),
            pltpu.VMEM((4, nq, hot_slots, 2 * span), bf16),
            pltpu.VMEM((4, nq, hot_slots, 3 * width), f32),
            pltpu.VMEM((nq, 4, hot_slots, 3 * width), f32),
            pltpu.VMEM((4 * hot_slots, 3 * width), bf16),
            pltpu.VMEM((rows, width), bf16),
            pltpu.VMEM((rows, width), bf16),
            pltpu.VMEM((width, rows), bf16),
            pltpu.VMEM((pieces, 4 * nq, nz, wide), bf16),
            pltpu.VMEM((3, 4 * nq * nz, width), f32),
            dma((steps, nz - 1)),
            dma((steps, nz - 1)),
            dma((steps, nq - 1)),
            dma((steps, nq - 1)),
            dma((steps, 2)),
            dma((steps, nq, 2)),
            dma((steps, nq, 2)),
            dma((steps, nq)),
            dma((steps, nq)),
            dma((3,)),
            dma((3,)),
            dma((nx - 1, 2)),
            dma((nx - 1, 2)),
            dma((nz - 1, 2)),
            dma((nz - 1, 2)),
            dma((nz - 1, 2)),
            dma((nz - 1, 2)),
            dma((nq - 1,)),
            dma((nq - 1,)),
            dma((3,)),
            dma((3,)),
            dma((nq - 1,)),
            dma((nq - 1,)),
            dma((nz - 1,)),
            dma((nz - 1,)),
            dma((nx - 1,)),
            dma((nx - 1,)),
            dma((1,)),
            dma((1,)),
            dma((16,)),
        ],
        compiler_params=pltpu.CompilerParams(
            collective_id=0, has_side_effects=True, vmem_limit_bytes=48 * 1024 * 1024
        ),
        cost_estimate=pl.CostEstimate(flops=0, bytes_accessed=300_000_000, transcendentals=0),
    )(send, send_hot, hot_rows, hot_at, w_gate, w_up, w_down)


def on_device(tokens, cotangent, gate_scale, expert_index, hot_index, w_gate, w_up, w_down):
    tok_rows, feature_width = tokens.shape
    experts = lax.axis_size("expert")
    nx, nc = 4, 2
    nq = nx * nc
    nz = experts // nq
    capacity = 3 * tok_rows // (2 * experts)
    hot_slots = 8
    hot_expert = hot_index[0]
    route_grad = (gate_scale[:, None] * cotangent.astype(jnp.float32)).astype(jnp.bfloat16)
    both = jnp.concatenate([tokens, route_grad], axis=1)
    is_hot = expert_index == hot_expert
    not_hot = jnp.logical_not(is_hot)
    owners = lax.broadcasted_iota(jnp.int32, (tok_rows, experts), 1)
    member = ((expert_index[:, None] == owners) & not_hot[:, None]).astype(jnp.int32)
    bucket_place = jnp.sum((jnp.cumsum(member, axis=0) - 1) * member, axis=1)
    slot_index = bucket_place * experts + expert_index
    slot_grid = lax.broadcasted_iota(jnp.int32, (experts * capacity, tok_rows), 0)
    cold_map = ((slot_grid == slot_index[None, :]) & not_hot[None, :]).astype(jnp.bfloat16)
    hot_place = jnp.cumsum(is_hot.astype(jnp.int32)) - 1
    hot_grid = lax.broadcasted_iota(jnp.int32, (hot_slots, tok_rows), 0)
    hot_map = ((hot_grid == hot_place[None, :]) & is_hot[None, :]).astype(jnp.bfloat16)
    send = route_rows(cold_map, both)
    own_hot = route_rows(hot_map, both)
    part = feature_width // experts
    hot_width = -(-2 * part // 128) * 128
    send_hot = jnp.concatenate(
        [
            own_hot[:, :feature_width].reshape(hot_slots, experts, part),
            own_hot[:, feature_width:].reshape(hot_slots, experts, part),
            jnp.zeros((hot_slots, experts, hot_width - 2 * part), jnp.bfloat16),
        ],
        axis=2,
    ).transpose(1, 0, 2)
    width = 2 * feature_width // PIECES
    half = feature_width // nc
    tile = half // 14
    hot_rows = jnp.stack(
        [
            jnp.concatenate(
                [
                    jnp.concatenate(
                        [
                            own_hot[:, at : at + (3 + x % 2) * tile],
                            jnp.zeros((hot_slots, (1 - x % 2) * tile), jnp.bfloat16),
                        ],
                        axis=1,
                    )
                    for at in (
                        c * half + (7 * x // 2) * tile,
                        feature_width + c * half + (7 * x // 2) * tile,
                    )
                ],
                axis=1,
            )
            for x in range(nx)
            for c in range(nc)
        ]
    )
    hot_at = jnp.stack([hot_expert // nq, hot_expert % nq // nc, hot_expert % nc])
    got, got_hot, hot_terms, hidden, gate_grad, up_grad = exchange(
        send.reshape(capacity, nz, nq, PIECES, width),
        send_hot.reshape(nz, nq, hot_slots, hot_width),
        hot_rows,
        hot_at,
        w_gate[0],
        w_up[0],
        w_down[0],
        nz,
        nx,
        nc,
    )
    rows = got.reshape(PIECES, capacity * 4 * experts, width)
    cold_tokens, cold_grads = rows[: PIECES // 2], rows[PIECES // 2 :]
    f32 = jnp.float32
    grad_gate = lax.dot_general(
        cold_tokens, gate_grad, (((1,), (0,)), ((), ())), preferred_element_type=f32
    ).astype(jnp.bfloat16).reshape(feature_width, -1)
    grad_up = lax.dot_general(
        cold_tokens, up_grad, (((1,), (0,)), ((), ())), preferred_element_type=f32
    ).astype(jnp.bfloat16).reshape(feature_width, -1)
    grad_down = jnp.concatenate(
        [column_sum(hidden, cold_grads[n]).astype(jnp.bfloat16) for n in range(PIECES // 2)],
        axis=1,
    )
    ff = w_gate.shape[2]
    hot_total = experts * 4 * hot_slots
    sums = column_sum(
        got_hot.reshape(hot_total, hot_width), hot_terms.reshape(hot_total, 3 * ff)
    )
    hot_grads = jnp.stack(
        [sums[:part, :ff], sums[:part, ff : 2 * ff], sums[part : 2 * part, 2 * ff :]], axis=1
    ).astype(jnp.bfloat16)[None]
    return (grad_gate[None], grad_up[None], grad_down[None], hot_grads)


def solution(mesh):
    placed = (
        P(("dp", "expert"), None),
        P(("dp", "expert"), None),
        P(("dp", "expert")),
        P(("dp", "expert")),
        P(),
        P("expert", None, "dp"),
        P("expert", None, "dp"),
        P("expert", "dp", None),
    )
    return jax.shard_map(
        on_device,
        mesh=mesh,
        in_specs=placed,
        out_specs=(
            P("expert", None, "dp"),
            P("expert", None, "dp"),
            P("expert", "dp", None),
            P(None, "expert", None, "dp"),
        ),
        check_vma=False,
    )
```

```python
import jax
import jax.numpy as jnp
from jax import lax
from jax.experimental import pallas as pl
from jax.experimental.pallas import tpu as pltpu
from jax.sharding import PartitionSpec as P

CONTRACT_ROWS = (((0,), (0,)), ((), ()))
MESH = pl.DeviceIdType.MESH
PIECES = 8


def terms_of(pre_gate, pre_up, hidden_back):
    sigmoid_gate = jax.nn.sigmoid(pre_gate)
    activated = pre_gate * sigmoid_gate
    hidden = (activated * pre_up).astype(jnp.bfloat16)
    gate_grad = (
        hidden_back * pre_up * sigmoid_gate * (1.0 + pre_gate * (1.0 - sigmoid_gate))
    ).astype(jnp.bfloat16)
    up_grad = (hidden_back * activated).astype(jnp.bfloat16)
    return (hidden, gate_grad, up_grad)


def column_sum(left, right):
    return lax.dot_general(left, right, CONTRACT_ROWS, preferred_element_type=jnp.float32)


def route_rows(selector, values):
    return jnp.dot(selector, values, preferred_element_type=jnp.float32).astype(jnp.bfloat16)


def exchange_kernel(nz, nx, nc, send, send_hot, hot_rows, hot_at, w_gate, w_up, w_down,
                    got, got_hot, hot_terms, cold_hidden, cold_gate, cold_up,
                    mid, mid_hot, turned, pair_gu, pair_d, one_gu, one_d, row_gu, row_d,
                    two_gu, two_d, col_gu, col_d, three_gu, three_d, full_gu, full_d,
                    hot_in, part, parts, own_terms,
                    gate_here, up_here, down_here, slot_rows, sums,
                    z_send, z_recv, q_send, q_recv, local_sem,
                    y_send, y_recv, f_send, f_recv,
                    c_send, c_recv, x_send, x_recv, w_send, w_recv, g_send, g_recv,
                    r_send, r_recv, v_send, v_recv, p_send, p_recv,
                    t_send, t_recv, u_send, u_recv, b_send, b_recv, own_sem):
    ny = 4
    nq = nx * nc
    chunks = send.shape[0]
    pieces = send.shape[3]
    group = 4
    y = lax.axis_index("dp")
    e = lax.axis_index("expert")
    z = lax.div(e, nq)
    q = lax.rem(e, nq)
    x = lax.div(q, nc)
    c = lax.rem(q, nc)
    up = lax.rem(y + 1, ny)
    down = lax.rem(y + ny - 1, ny)
    twin = (y, z * nq + x * nc + (1 - c))
    half = w_gate.shape[0] // nc
    width = w_gate.shape[1]
    span = one_gu.shape[1] // 14 * 4
    z_rows = span // nz
    d_rows = width // nz

    def z_peer(k):
        return lax.rem(z + k, nz)

    def q_peer(k):
        return lax.rem(q + k, nq)

    def q_source(k):
        return lax.rem(q + nq - k, nq)

    def x_peer(k):
        return lax.rem(x + k, nx)

    def z_dev(k):
        return (y, z_peer(k) * nq + q)

    def q_dev(k):
        return (y, z * nq + q_peer(k))

    def x_dev(k):
        return (y, z * nq + x_peer(k) * nc + c)

    def remote(src, dst, send_sem, recv_sem, device):
        return pltpu.make_async_remote_copy(
            src_ref=src, dst_ref=dst, send_sem=send_sem, recv_sem=recv_sem,
            device_id=device, device_id_type=MESH)

    barrier = pltpu.get_barrier_semaphore()
    for k in range(1, nz):
        pl.semaphore_signal(barrier, inc=1, device_id=z_dev(k), device_id_type=MESH)
    for k in range(1, nq):
        pl.semaphore_signal(barrier, inc=1, device_id=q_dev(k), device_id_type=MESH)
    for k in range(1, ny):
        pl.semaphore_signal(barrier, inc=1, device_id=(lax.rem(y + k, ny), e), device_id_type=MESH)
    pl.semaphore_wait(barrier, nz - 1 + nq - 1 + ny - 1)

    def z_refs(s):
        if s < chunks:
            return send.at[s], mid.at[s]
        return send_hot, mid_hot

    def q_dst(s, who):
        if s < chunks:
            return got.at[:, (s * ny + y) * nq + who]
        return got_hot.at[:, who, y]

    def y_block(s, who, plane):
        if s < chunks:
            return got.at[:, (s * ny + plane) * nq + who]
        return got_hot.at[:, who, plane]

    def z_copy(s, k):
        src, dst = z_refs(s)
        return remote(src.at[z_peer(k)], dst.at[z], z_send.at[s, k - 1], z_recv.at[s, k - 1], z_dev(k))

    def z_own(s):
        src, dst = z_refs(s)
        return pltpu.make_async_copy(src.at[z], dst.at[z], local_sem.at[s, 0])

    def q_src(s, who):
        if s < chunks:
            return turned.at[s, who]
        return mid_hot.at[:, who]

    def q_copy(s, k):
        return remote(q_src(s, q_peer(k)), q_dst(s, q), q_send.at[s, k - 1], q_recv.at[s, k - 1], q_dev(k))

    def q_own(s):
        return pltpu.make_async_copy(q_src(s, q), q_dst(s, q), local_sem.at[s, 1])

    def y_copy(s, k, way):
        block = y_block(s, q_source(k), y)
        return remote(block, block, y_send.at[s, k, way], y_recv.at[s, k, way],
                      (up if way == 0 else down, e))

    def f_copy(s, k):
        way = 0 if k < nq // 2 else 1
        block = y_block(s, q_source(k), down if way == 0 else up)
        return remote(block, block, f_send.at[s, k], f_recv.at[s, k],
                      (up if way == 0 else down, e))

    z_order = sorted(range(1, nz), key=lambda k: -min(k, nz - k))

    def start_z(s):
        z_own(s).start()
        for k in z_order:
            z_copy(s, k).start()

    def pass_on(s, k):
        way = 0 if k < nq // 2 else 1
        y_copy(s, k, way).wait_recv()
        f_copy(s, k).start()

    block_rows = nz * group * pieces
    to_row = lax.broadcasted_iota(jnp.int32, (block_rows, block_rows), 0)
    from_row = lax.broadcasted_iota(jnp.int32, (block_rows, block_rows), 1)
    wanted = (
        (to_row % nz) * (group * pieces)
        + (to_row // (pieces * nz)) * pieces
        + (to_row // nz) % pieces
    )
    turn_map = jnp.where(from_row == wanted, 1.0, 0.0).astype(jnp.bfloat16)

    def turn(s):
        for g in range(nq // group):
            block = mid[s, :, g * group : (g + 1) * group].astype(jnp.float32)
            block = block.reshape(block_rows, block.shape[-1]).astype(jnp.bfloat16)
            moved = jnp.dot(turn_map, block, preferred_element_type=jnp.float32)
            turned[s, g * group : (g + 1) * group] = moved.reshape(
                group, pieces, nz, moved.shape[-1]).astype(jnp.bfloat16)

    def run_chunk(s, passing=True):
        z_own(s).wait()
        for k in z_order:
            z_copy(s, k).wait_recv()
        if s < chunks:
            turn(s)
        q_own(s).start()
        for k in range(1, nq):
            q_copy(s, k).start()
        for k in range(nq):
            if k == 0:
                q_own(s).wait()
            else:
                q_copy(s, k).wait_recv()
            y_copy(s, k, 0).start()
            y_copy(s, k, 1).start()
            if s > 0 and passing:
                pass_on(s - 1, k)

    def row_half(who):
        return pl.ds(pl.multiple_of(who * half, half), half)

    def c_copies(who):
        return (
            (w_gate.at[row_half(who), :], pair_gu.at[c, 0]),
            (w_up.at[row_half(who), :], pair_gu.at[c, 1]),
            (w_down.at[:, row_half(who)], pair_d.at[c]),
        )

    def c_copy(i):
        src, dst = c_copies(1 - c)[i]
        return remote(src, dst, c_send.at[i], c_recv.at[i], twin)

    def c_own(i):
        src, dst = c_copies(c)[i]
        return pltpu.make_async_copy(src, dst, own_sem.at[i])

    def x_span(who):
        first = who * 3 + lax.div(who, 2)
        return pl.ds(pl.multiple_of(first * (half // 14), half // 14), span)

    def x_pair(who):
        return (
            (one_gu.at[:, x_span(who), :], row_gu.at[x]),
            (one_d.at[:, x_span(who)], row_d.at[x]),
        )

    def x_copy(k, i):
        src, dst = x_pair(x_peer(k))[i]
        return remote(src, dst, x_send.at[k - 1, i], x_recv.at[k - 1, i], x_dev(k))

    def x_own(i):
        src, dst = x_pair(x)[i]
        return pltpu.make_async_copy(src, dst, own_sem.at[3 + i])

    def z_part(who):
        return pl.ds(pl.multiple_of(who * z_rows, z_rows), z_rows)

    def d_part(who):
        return pl.ds(pl.multiple_of(who * d_rows, d_rows), d_rows)

    def w_pair(who):
        return (
            (two_gu.at[:, z_part(who), :], col_gu.at[z]),
            (two_d.at[d_part(who), :], col_d.at[z]),
        )

    def w_copy(k, i):
        src, dst = w_pair(z_peer(k))[i]
        return remote(src, dst, w_send.at[k - 1, i], w_recv.at[k - 1, i], z_dev(k))

    def w_own(i):
        src, dst = w_pair(z)[i]
        return pltpu.make_async_copy(src, dst, own_sem.at[5 + i])

    g_pair = (
        (three_gu, full_gu.at[:, z_part(z), :]),
        (three_d, full_d.at[d_part(z), :]),
    )

    def g_copy(k, i):
        src, dst = g_pair[i]
        return remote(src, dst, g_send.at[k - 1, i], g_recv.at[k - 1, i], z_dev(k))

    def g_own(i):
        src, dst = g_pair[i]
        return pltpu.make_async_copy(src, dst, own_sem.at[7 + i])

    def r_copy(k):
        return remote(hot_rows.at[q_peer(k)], hot_in.at[y, q], r_send.at[k - 1], r_recv.at[k - 1], q_dev(k))

    r_own = pltpu.make_async_copy(hot_rows.at[q], hot_in.at[y, q], own_sem.at[9])

    def v_copy(k):
        return remote(hot_in.at[y], hot_in.at[y], v_send.at[k - 1], v_recv.at[k - 1],
                      (lax.rem(y + k, ny), e))

    def p_copy(k):
        return remote(part.at[:, q_peer(k)], parts.at[q], p_send.at[k - 1], p_recv.at[k - 1], q_dev(k))

    p_own = pltpu.make_async_copy(part.at[:, q], parts.at[q], own_sem.at[10])

    def t_copy(k):
        return remote(own_terms, hot_terms.at[z, x, c], t_send.at[k - 1], t_recv.at[k - 1], z_dev(k))

    t_own = pltpu.make_async_copy(own_terms, hot_terms.at[z, x, c], own_sem.at[11])

    def u_copy(k):
        block = hot_terms.at[:, x, c]
        return remote(block, block, u_send.at[k - 1], u_recv.at[k - 1], x_dev(k))

    def b_copy():
        block = hot_terms.at[:, :, c]
        return remote(block, block, b_send.at[0], b_recv.at[0], twin)

    here = ((w_gate, gate_here), (w_up, up_here), (w_down, down_here))

    def here_copy(i):
        return pltpu.make_async_copy(here[i][0], here[i][1], own_sem.at[12 + i])

    def cold(s):
        for k in range(nq):
            y_copy(s, k, 1 if k < nq // 2 else 0).wait_recv()
            f_copy(s, k).wait_recv()
        tiles = ny * nq
        taken = pltpu.make_async_copy(
            got.at[:, s * tiles : (s + 1) * tiles], slot_rows, own_sem.at[15])
        taken.start()
        taken.wait()
        step = slot_rows.shape[-1]
        count = tiles * nz

        def piece(n):
            block = slot_rows[n].astype(jnp.float32)
            return block.reshape(count, step).astype(jnp.bfloat16)

        for n in range(pieces // 2):
            cut = slice(n * step, (n + 1) * step)
            row_tokens, row_grads = piece(n), piece(pieces // 2 + n)
            new = (
                jnp.dot(row_tokens, gate_here[cut, :], preferred_element_type=jnp.float32),
                jnp.dot(row_tokens, up_here[cut, :], preferred_element_type=jnp.float32),
                lax.dot_general(row_grads, down_here[:, cut], (((1,), (1,)), ((), ())),
                                preferred_element_type=jnp.float32),
            )
            for m in range(3):
                if n == 0:
                    sums[m] = new[m]
                else:
                    sums[m] += new[m]
        hidden, gate_grad, up_grad = terms_of(sums[0], sums[1], sums[2])
        at = slice(s * count, (s + 1) * count)
        cold_hidden[at, :] = hidden
        cold_gate[at, :] = gate_grad
        cold_up[at, :] = up_grad

    hot_z = hot_at[0]
    hot_x = hot_at[1]
    hot_c = hot_at[2]

    for i in range(3):
        c_copy(i).start()
        c_own(i).start()
    r_own.start()
    for k in range(1, nq):
        r_copy(k).start()
    start_z(0)
    start_z(chunks)
    start_z(1)
    start_z(2)
    for i in range(3):
        c_own(i).wait()
        c_copy(i).wait_recv()

    for i in range(3):
        here_copy(i).start()
    tile = half // 14

    def keep_half(n, carry):
        rows = pl.ds(pl.multiple_of(n * tile, tile), tile)
        one_gu[0, rows, :] = pair_gu[hot_c, 0, rows, :]
        one_gu[1, rows, :] = pair_gu[hot_c, 1, rows, :]
        one_d[:, rows] = pair_d[hot_c, :, rows]
        return carry

    lax.fori_loop(0, 14, keep_half, 0)
    for i in range(2):
        x_own(i).start()
        for k in range(1, nx):
            x_copy(k, i).start()

    r_own.wait()
    for k in range(1, nq):
        r_copy(k).wait_recv()
    for k in range(1, ny):
        v_copy(k).start()

    run_chunk(0)

    for i in range(2):
        x_own(i).wait()
        for k in range(1, nx):
            x_copy(k, i).wait_recv()
    two_gu[...] = row_gu[hot_x]
    two_d[...] = row_d[hot_x]
    for i in range(2):
        w_own(i).start()
        for k in z_order:
            w_copy(k, i).start()

    run_chunk(1)

    for i in range(2):
        w_own(i).wait()
        for k in z_order:
            w_copy(k, i).wait_recv()
    three_gu[...] = col_gu[hot_z]
    three_d[...] = col_d[hot_z]
    for i in range(2):
        g_own(i).start()
        for k in z_order:
            g_copy(k, i).start()

    run_chunk(2)

    for k in range(1, ny):
        v_copy(k).wait_recv()
    for i in range(2):
        g_own(i).wait()
        for k in z_order:
            g_copy(k, i).wait_recv()
    rows = hot_in[...].astype(jnp.float32).reshape(ny * nq * 8, 2 * span).astype(jnp.bfloat16)
    row_tokens, row_grads = rows[:, :span], rows[:, span:]
    flat = (ny, nq, 8, width)
    part[:, :, :, 0:width] = jnp.dot(
        row_tokens, full_gu[0], preferred_element_type=jnp.float32).reshape(flat)
    part[:, :, :, width : 2 * width] = jnp.dot(
        row_tokens, full_gu[1], preferred_element_type=jnp.float32).reshape(flat)
    part[:, :, :, 2 * width :] = lax.dot_general(
        row_grads, full_d[...], (((1,), (1,)), ((), ())),
        preferred_element_type=jnp.float32).reshape(flat)
    p_own.start()
    for k in range(1, nq):
        p_copy(k).start()

    run_chunk(chunks, False)

    p_own.wait()
    for k in range(1, nq):
        p_copy(k).wait_recv()
    total = parts[0]
    for k in range(1, nq):
        total = total + parts[k]
    total = total.reshape(ny * 8, 3 * width)
    pre_gate, pre_up, hidden_back = (
        total[:, :width], total[:, width : 2 * width], total[:, 2 * width :])
    hidden, gate_grad, up_grad = terms_of(pre_gate, pre_up, hidden_back)
    own_terms[:, 0:width] = gate_grad
    own_terms[:, width : 2 * width] = up_grad
    own_terms[:, 2 * width :] = hidden
    t_own.start()
    for k in z_order:
        t_copy(k).start()

    for k in range(nq):
        pass_on(2, k)
    t_own.wait()
    for k in z_order:
        t_copy(k).wait_recv()
    for k in range(1, nx):
        u_copy(k).start()
    for k in range(nq):
        pass_on(chunks, k)
    for i in range(3):
        here_copy(i).wait()
    cold(0)
    cold(1)
    for k in range(1, nx):
        u_copy(k).wait_recv()
    b_copy().start()
    cold(2)
    b_copy().wait()

    for i in range(3):
        c_copy(i).wait_send()
    for k in range(1, nx):
        u_copy(k).wait_send()
        for i in range(2):
            x_copy(k, i).wait_send()
    for k in range(1, nz):
        t_copy(k).wait_send()
        for i in range(2):
            w_copy(k, i).wait_send()
            g_copy(k, i).wait_send()
    for k in range(1, ny):
        v_copy(k).wait_send()
    for k in range(1, nq):
        r_copy(k).wait_send()
        p_copy(k).wait_send()
    for s in range(chunks + 1):
        for k in range(1, nz):
            z_copy(s, k).wait_send()
        for k in range(1, nq):
            q_copy(s, k).wait_send()
        for k in range(nq):
            y_copy(s, k, 0).wait_send()
            y_copy(s, k, 1).wait_send()
            f_copy(s, k).wait_send()
            if s == chunks:
                y_copy(s, k, 1 if k < nq // 2 else 0).wait_recv()
                f_copy(s, k).wait_recv()


def exchange(send, send_hot, hot_rows, hot_at, w_gate, w_up, w_down, nz, nx, nc):
    slots, _, nq, pieces, wide = send.shape
    hot_slots, hot_width = send_hot.shape[-2:]
    bf16, f32 = jnp.bfloat16, jnp.float32
    steps = slots + 1
    dma = pltpu.SemaphoreType.DMA
    rows, width = w_gate.shape
    half = rows // nc
    span = half // 14 * 4

    def body(*refs):
        exchange_kernel(nz, nx, nc, *refs)

    hbm = pl.BlockSpec(memory_space=pl.ANY)
    vmem = pl.BlockSpec(memory_space=pltpu.VMEM)
    smem = pl.BlockSpec(memory_space=pltpu.SMEM)
    return pl.pallas_call(
        body,
        out_shape=(
            jax.ShapeDtypeStruct((pieces, slots * 4 * nq, nz, wide), bf16),
            jax.ShapeDtypeStruct((nz, nq, 4, hot_slots, hot_width), bf16),
            jax.ShapeDtypeStruct((nz, nx, nc, 4 * hot_slots, 3 * width), bf16),
            jax.ShapeDtypeStruct((slots * 4 * nq * nz, width), bf16),
            jax.ShapeDtypeStruct((slots * 4 * nq * nz, width), bf16),
            jax.ShapeDtypeStruct((slots * 4 * nq * nz, width), bf16),
        ),
        in_specs=[hbm, hbm, vmem, smem, hbm, hbm, hbm],
        out_specs=(hbm, hbm, hbm, vmem, vmem, vmem),
        scratch_shapes=[
            pltpu.VMEM((slots, nz, nq, pieces, wide), bf16),
            pltpu.VMEM((nz, nq, hot_slots, hot_width), bf16),
            pltpu.VMEM((slots, nq, pieces, nz, wide), bf16),
            pltpu.VMEM((nc, 2, half, width), bf16),
            pltpu.VMEM((nc, width, half), bf16),
            pltpu.VMEM((2, half, width), bf16),
            pltpu.VMEM((width, half), bf16),
            pltpu.VMEM((nx, 2, span, width), bf16),
            pltpu.VMEM((nx, width, span), bf16),
            pltpu.VMEM((2, span, width), bf16),
            pltpu.VMEM((width, span), bf16),
            pltpu.VMEM((nz, 2, span // nz, width), bf16),
            pltpu.VMEM((nz, width // nz, span), bf16),
            pltpu.VMEM((2, span // nz, width), bf16),
            pltpu.VMEM((width // nz, span), bf16),
            pltpu.VMEM((2, span, width), bf16),
            pltpu.VMEM((width, span), bf16),
            pltpu.VMEM((4, nq, hot_slots, 2 * span), bf16),
            pltpu.VMEM((4, nq, hot_slots, 3 * width), f32),
            pltpu.VMEM((nq, 4, hot_slots, 3 * width), f32),
            pltpu.VMEM((4 * hot_slots, 3 * width), bf16),
            pltpu.VMEM((rows, width), bf16),
            pltpu.VMEM((rows, width), bf16),
            pltpu.VMEM((width, rows), bf16),
            pltpu.VMEM((pieces, 4 * nq, nz, wide), bf16),
            pltpu.VMEM((3, 4 * nq * nz, width), f32),
            dma((steps, nz - 1)),
            dma((steps, nz - 1)),
            dma((steps, nq - 1)),
            dma((steps, nq - 1)),
            dma((steps, 2)),
            dma((steps, nq, 2)),
            dma((steps, nq, 2)),
            dma((steps, nq)),
            dma((steps, nq)),
            dma((3,)),
            dma((3,)),
            dma((nx - 1, 2)),
            dma((nx - 1, 2)),
            dma((nz - 1, 2)),
            dma((nz - 1, 2)),
            dma((nz - 1, 2)),
            dma((nz - 1, 2)),
            dma((nq - 1,)),
            dma((nq - 1,)),
            dma((3,)),
            dma((3,)),
            dma((nq - 1,)),
            dma((nq - 1,)),
            dma((nz - 1,)),
            dma((nz - 1,)),
            dma((nx - 1,)),
            dma((nx - 1,)),
            dma((1,)),
            dma((1,)),
            dma((16,)),
        ],
        compiler_params=pltpu.CompilerParams(
            collective_id=0, has_side_effects=True, vmem_limit_bytes=36 * 1024 * 1024
        ),
        cost_estimate=pl.CostEstimate(flops=0, bytes_accessed=300_000_000, transcendentals=0),
    )(send, send_hot, hot_rows, hot_at, w_gate, w_up, w_down)


def on_device(tokens, cotangent, gate_scale, expert_index, hot_index, w_gate, w_up, w_down):
    tok_rows, feature_width = tokens.shape
    experts = lax.axis_size("expert")
    nx, nc = 4, 2
    nq = nx * nc
    nz = experts // nq
    capacity = 3 * tok_rows // (2 * experts)
    hot_slots = 8
    hot_expert = hot_index[0]
    route_grad = (gate_scale[:, None] * cotangent.astype(jnp.float32)).astype(jnp.bfloat16)
    both = jnp.concatenate([tokens, route_grad], axis=1)
    is_hot = expert_index == hot_expert
    not_hot = jnp.logical_not(is_hot)
    owners = lax.broadcasted_iota(jnp.int32, (tok_rows, experts), 1)
    member = ((expert_index[:, None] == owners) & not_hot[:, None]).astype(jnp.int32)
    bucket_place = jnp.sum((jnp.cumsum(member, axis=0) - 1) * member, axis=1)
    slot_index = bucket_place * experts + expert_index
    slot_grid = lax.broadcasted_iota(jnp.int32, (experts * capacity, tok_rows), 0)
    cold_map = ((slot_grid == slot_index[None, :]) & not_hot[None, :]).astype(jnp.bfloat16)
    hot_place = jnp.cumsum(is_hot.astype(jnp.int32)) - 1
    hot_grid = lax.broadcasted_iota(jnp.int32, (hot_slots, tok_rows), 0)
    hot_map = ((hot_grid == hot_place[None, :]) & is_hot[None, :]).astype(jnp.bfloat16)
    send = route_rows(cold_map, both)
    own_hot = route_rows(hot_map, both)
    part = feature_width // experts
    hot_width = -(-2 * part // 128) * 128
    send_hot = jnp.concatenate(
        [
            own_hot[:, :feature_width].reshape(hot_slots, experts, part),
            own_hot[:, feature_width:].reshape(hot_slots, experts, part),
            jnp.zeros((hot_slots, experts, hot_width - 2 * part), jnp.bfloat16),
        ],
        axis=2,
    ).transpose(1, 0, 2)
    width = 2 * feature_width // PIECES
    half = feature_width // nc
    tile = half // 14
    hot_rows = jnp.stack(
        [
            jnp.concatenate(
                [
                    jnp.concatenate(
                        [
                            own_hot[:, at : at + (3 + x % 2) * tile],
                            jnp.zeros((hot_slots, (1 - x % 2) * tile), jnp.bfloat16),
                        ],
                        axis=1,
                    )
                    for at in (
                        c * half + (7 * x // 2) * tile,
                        feature_width + c * half + (7 * x // 2) * tile,
                    )
                ],
                axis=1,
            )
            for x in range(nx)
            for c in range(nc)
        ]
    )
    hot_at = jnp.stack([hot_expert // nq, hot_expert % nq // nc, hot_expert % nc])
    got, got_hot, hot_terms, hidden, gate_grad, up_grad = exchange(
        send.reshape(capacity, nz, nq, PIECES, width),
        send_hot.reshape(nz, nq, hot_slots, hot_width),
        hot_rows,
        hot_at,
        w_gate[0],
        w_up[0],
        w_down[0],
        nz,
        nx,
        nc,
    )
    rows = got.reshape(PIECES, capacity * 4 * experts, width)
    cold_tokens, cold_grads = rows[: PIECES // 2], rows[PIECES // 2 :]
    f32 = jnp.float32
    grad_gate = lax.dot_general(
        cold_tokens, gate_grad, (((1,), (0,)), ((), ())), preferred_element_type=f32
    ).astype(jnp.bfloat16).reshape(feature_width, -1)
    grad_up = lax.dot_general(
        cold_tokens, up_grad, (((1,), (0,)), ((), ())), preferred_element_type=f32
    ).astype(jnp.bfloat16).reshape(feature_width, -1)
    grad_down = jnp.concatenate(
        [column_sum(hidden, cold_grads[n]).astype(jnp.bfloat16) for n in range(PIECES // 2)],
        axis=1,
    )
    ff = w_gate.shape[2]
    hot_total = experts * 4 * hot_slots
    sums = column_sum(
        got_hot.reshape(hot_total, hot_width), hot_terms.reshape(hot_total, 3 * ff)
    )
    hot_grads = jnp.stack(
        [sums[:part, :ff], sums[:part, ff : 2 * ff], sums[part : 2 * part, 2 * ff :]], axis=1
    ).astype(jnp.bfloat16)[None]
    return (grad_gate[None], grad_up[None], grad_down[None], hot_grads)


def solution(mesh):
    placed = (
        P(("dp", "expert"), None),
        P(("dp", "expert"), None),
        P(("dp", "expert")),
        P(("dp", "expert")),
        P(),
        P("expert", None, "dp"),
        P("expert", None, "dp"),
        P("expert", "dp", None),
    )
    return jax.shard_map(
        on_device,
        mesh=mesh,
        in_specs=placed,
        out_specs=(
            P("expert", None, "dp"),
            P("expert", None, "dp"),
            P("expert", "dp", None),
            P(None, "expert", None, "dp"),
        ),
        check_vma=False,
    )
```
